128 devices in a mesh: party: 2 (over x_hi), dp: 64 (over y, x_lo, z, core).
Axes of the slice: x: 4 (x_hi: 2, x_lo: 2; x = x_hi * 2 + x_lo), y: 4, z: 4, core: 2. Of those that a mesh axis runs over, the one named last changes fastest.
Arguments:
- x_share: float32 [2, 32768, 1024], P('party', 'dp'), may hold values from -6 to 6
- w_share: float32 [2, 1024, 2048], P('party', 'dp'), may hold values from -0.1875 to 0.1875
- g_share: float32 [2, 32768, 2048], P('party', 'dp'), may hold values from -0.03125 to 0.03125
- fwd_a: float32 [2, 32768, 1024], P('party', 'dp'), may hold values from -4 to 4
- fwd_b: float32 [2, 1024, 2048], P('party', 'dp'), may hold values from -0.125 to 0.125
- fwd_c: float32 [2, 32768, 2048], P('party', 'dp'), may hold values from -2100 to 2100, as said below
- bwd_a: float32 [2, 32768, 1024], P('party', 'dp'), may hold values from -4 to 4
- bwd_b: float32 [2, 32768, 2048], P('party', 'dp'), may hold values from -0.022097087 to 0.022097087
- bwd_c: float32 [2, 1024, 2048], P('party', 'dp'), may hold values from -2100 to 2100, as said below
Outputs:
- y_share: float32 [2, 32768, 2048], P('party', 'dp')
- dw_share: float32 [2, 1024, 2048], P('party', 'dp')
The draws below stay inside these ranges and needn't reach their ends.
Inputs may be any that keep to these rules, and one draw needn't show every extreme that they name: fwd_c[0] + fwd_c[1] equals (fwd_a[0] + fwd_a[1]) (fwd_b[0] + fwd_b[1]) up to float32 rounding. bwd_c[0] + bwd_c[1] equals (bwd_a[0] + bwd_a[1])^T (bwd_b[0] + bwd_b[1]) up to float32 rounding.
All inputs are finite; a program needn't handle non-finite values.
Results may differ from the reference program's by a relative error of at most 0.0001.
Values sent between devices are 32-bit elements; how exact they have to be, the bound alone decides.
No kernel may reach another device: no remote copies, remote signals or barrier semaphores. Data moves between devices by JAX's collectives and lax.ppermute only.
A program may use at most 128 MiB of HBM per device.

```python
import jax
import jax.numpy as jnp
from jax import lax

D = 1024
FF = 2048
TOKENS = 32768


def factor_left(key, salt):
    return jnp.clip(jax.random.normal(jax.random.fold_in(key, salt), (2, TOKENS, D), jnp.float32), -4.0, 4.0)


def forward_right(key):
    values = jnp.clip(jax.random.normal(jax.random.fold_in(key, 21), (2, D, FF), jnp.float32), -4.0, 4.0)
    return values * (1.0 / 32.0)


def backward_right(key):
    values = jnp.clip(jax.random.normal(jax.random.fold_in(key, 31), (2, TOKENS, FF), jnp.float32), -4.0, 4.0)
    return values * (1.0 / TOKENS) ** 0.5


def draw_fwd_a(key, part):
    return factor_left(key, 11)


def draw_fwd_b(key, part):
    return forward_right(key)


def draw_fwd_c(key, part):
    left = factor_left(key, 11)
    right = forward_right(key)
    product = jnp.dot(left[0] + left[1], right[0] + right[1], precision=lax.Precision.HIGHEST, preferred_element_type=jnp.float32)
    masking = jnp.clip(jax.random.normal(jax.random.fold_in(key, 41), (TOKENS, FF), jnp.float32), -4.0, 4.0)
    return jnp.stack([product - masking, masking])


def draw_bwd_a(key, part):
    return factor_left(key, 13)


def draw_bwd_b(key, part):
    return backward_right(key)


def draw_bwd_c(key, part):
    left = factor_left(key, 13)
    right = backward_right(key)
    product = lax.dot_general(left[0] + left[1], right[0] + right[1], (((0,), (0,)), ((), ())), precision=lax.Precision.HIGHEST, preferred_element_type=jnp.float32)
    masking = jnp.clip(jax.random.normal(jax.random.fold_in(key, 43), (D, FF), jnp.float32), -4.0, 4.0)
    return jnp.stack([product - masking, masking])


def steps_of(rng, dims, cuts, smallest, largest):
    level = 1.0
    for dim, parts in cuts:
        draws = jax.random.uniform(jax.random.fold_in(jax.random.fold_in(rng, 6), dim), (parts,), jnp.float32, smallest / len(cuts), largest / len(cuts))
        level = level * jnp.repeat(jnp.exp(draws), dims[dim] // parts).reshape((-1,) + (1,) * (len(dims) - 1 - dim))
    return level


def noise(stream_key, extent, scale, limit, shards=(), held_as=jnp.bfloat16):
    level = steps_of(stream_key, extent, shards, -0.22, 0.18) if shards else 1.0
    drawn = jax.random.normal(stream_key, extent, jnp.float32) * scale * level
    return jnp.minimum(jnp.maximum(drawn, -limit), limit).astype(held_as)


def setup_inputs(seed: int = 0) -> dict:
    key_of = jax.random.split(jax.random.key(seed), 10)
    return {
        "x_share": noise(key_of[0], (2, TOKENS, D), 1.0, 6.0, ((0, 2), (1, 64)), jnp.float32),
        "w_share": noise(key_of[1], (2, D, FF), D ** -0.5, 0.1875, ((0, 2), (1, 64)), jnp.float32),
        "g_share": noise(key_of[2], (2, TOKENS, FF), TOKENS ** -0.5, 0.03125, ((0, 2), (1, 64)), jnp.float32),
        "fwd_a": draw_fwd_a(jax.random.fold_in(key_of[9], 71), 0),
        "fwd_b": draw_fwd_b(jax.random.fold_in(key_of[9], 71), 0),
        "fwd_c": draw_fwd_c(jax.random.fold_in(key_of[9], 71), 0),
        "bwd_a": draw_bwd_a(jax.random.fold_in(key_of[9], 71), 0),
        "bwd_b": draw_bwd_b(jax.random.fold_in(key_of[9], 71), 0),
        "bwd_c": draw_bwd_c(jax.random.fold_in(key_of[9], 71), 0),
    }


def matmul(left, right):
    return jnp.dot(left, right, preferred_element_type=jnp.float32, precision=lax.Precision.HIGHEST)


def tmatmul(left, right):
    return lax.dot_general(left, right, (((0,), (0,)), ((), ())), precision=lax.Precision.HIGHEST, preferred_element_type=jnp.float32)


def reference(x_share, w_share, g_share, fwd_a, fwd_b, fwd_c, bwd_a, bwd_b, bwd_c):
    eps_fwd = (x_share[0] - fwd_a[0]) + (x_share[1] - fwd_a[1])
    delta_fwd = (w_share[0] - fwd_b[0]) + (w_share[1] - fwd_b[1])
    eps_bwd = (x_share[0] - bwd_a[0]) + (x_share[1] - bwd_a[1])
    delta_bwd = (g_share[0] - bwd_b[0]) + (g_share[1] - bwd_b[1])
    outputs = []
    grads = []
    for party in range(2):
        first = jnp.float32(1.0 if party == 0 else 0.0)
        outputs.append(fwd_c[party] + matmul(eps_fwd, fwd_b[party] + first * delta_fwd) + matmul(fwd_a[party], delta_fwd))
        grads.append(bwd_c[party] + tmatmul(eps_bwd, bwd_b[party] + first * delta_bwd) + tmatmul(bwd_a[party], delta_bwd))
    return jnp.stack(outputs), jnp.stack(grads)
```

```python
import jax
import jax.numpy as jnp
from jax import lax
from jax.sharding import Mesh
from jax.sharding import PartitionSpec as P

DP = ("y", "xl", "z", "core")
SWAP = [(0, 1), (1, 0)]


def dot(left, right):
    return jnp.dot(left, right, preferred_element_type=jnp.float32, precision=lax.Precision.HIGH)


def after(value, *earlier):
    return lax.optimization_barrier((value, *earlier))[0]


def rows_of(share, core):
    t = share.T.reshape(4, 2, 4, 2, 16, share.shape[0])
    t = lax.dynamic_index_in_dim(t, core, 3, keepdims=False)
    return t.swapaxes(1, 2).reshape(-1, share.shape[0])


def body(x_share, w_share, g_share, fwd_a, fwd_b, fwd_c, bwd_a, bwd_b, bwd_c):
    x, w, g = x_share[0], w_share[0], g_share[0]
    fa, fb, fc = fwd_a[0], fwd_b[0], fwd_c[0]
    ba, bb, bc = bwd_a[0], bwd_b[0], bwd_c[0]
    party0 = lax.axis_index("party") == 0
    first = party0.astype(jnp.float32)
    core = lax.axis_index("core")
    rows = w.shape[0]
    ff = w.shape[1]

    d_rows = w - fb
    delta_rows = d_rows + lax.ppermute(d_rows, "party", SWAP)
    packed = jnp.concatenate([fb + first * delta_rows, delta_rows], axis=1)
    packed_x = lax.ppermute(packed, "xl", SWAP)
    xl0 = lax.axis_index("xl") == 0
    weights = jnp.concatenate(
        [jnp.where(xl0, packed, packed_x), jnp.where(xl0, packed_x, packed)], axis=1
    )
    weights = lax.all_gather(weights, ("y", "z", "core"), axis=0, tiled=True)

    x_mine, x_theirs = rows_of(x, core), rows_of(x, 1 - core)
    a_mine, a_theirs = rows_of(ba, core), rows_of(ba, 1 - core)
    x_other = lax.ppermute(x_theirs, "core", SWAP)
    a_other = lax.ppermute(a_theirs, "core", SWAP)
    r_mine = g - (1.0 - first) * bb
    r_other = lax.ppermute(r_mine, "core", SWAP)
    b_other = lax.ppermute(bb, "core", SWAP)

    xm = lax.ppermute(x_mine, "party", SWAP)
    xo = lax.ppermute(x_other, "party", SWAP)
    am = lax.ppermute(after(a_mine, xm), "party", [(1, 0)])
    ao = lax.ppermute(after(a_other, xo), "party", [(1, 0)])
    half = x.shape[0] // 2
    u = x - fa
    u0 = lax.ppermute(after(u[:half], am), "party", SWAP)
    u1 = lax.ppermute(after(u[half:], ao), "party", SWAP)

    opened = jnp.concatenate([x_mine + xm, x_other + xo], axis=1)
    a_local = jnp.concatenate([a_mine, a_other], axis=1)
    a_second = jnp.where(party0, jnp.concatenate([am, ao], axis=1), a_local)
    left_b = jnp.where(party0, a_local, opened)
    right = jnp.concatenate([r_mine, r_other], axis=0)
    right_b = jnp.concatenate([bb, b_other], axis=0)
    t3 = dot(left_b, right_b)
    part0 = dot(opened - a_second, right) - first * t3
    part1 = dot(a_second, right) + t3
    both = jnp.concatenate(
        [part0.reshape(16, 2 * rows, ff), part1.reshape(16, 2 * rows, ff)], axis=1
    )
    both = after(both, weights)
    both = lax.psum_scatter(both, ("y", "z"), scatter_dimension=0, tiled=True)
    both = both.reshape(2, 2, rows, ff)
    keep = jnp.where(xl0, both[:, 0], both[:, 1])
    give = jnp.where(xl0, both[:, 1], both[:, 0])
    both = keep + lax.ppermute(give, "xl", SWAP)
    give = jnp.where(party0, both[1] - bc, both[0])
    keep = jnp.where(party0, both[0] + bc, both[1])
    grad = keep + lax.ppermute(give, "party", SWAP)

    def columns(share, xl):
        return share.reshape(-1, 4, 2, 128)[:, :, xl].reshape(-1, 512)

    def outputs_of(eps, a, c):
        out = c
        for xl in range(2):
            at = xl * 2 * ff
            out = out + dot(columns(eps, xl), weights[:, at : at + ff])
            out = out + dot(columns(a, xl), weights[:, at + ff : at + 2 * ff])
        return out

    eps0, eps1 = u[:half] + u0, u[half:] + u1
    outputs = outputs_of(jnp.concatenate([eps0, eps1]), fa, fc)
    return (outputs[None], grad[None])


def solution(mesh):
    split = Mesh(
        mesh.devices.reshape(mesh.shape["party"], 4, 2, 4, 2),
        ("party", *DP),
    )
    spec = P("party", DP, None)
    return jax.shard_map(
        body, mesh=split, in_specs=(spec,) * 9, out_specs=(spec, spec), check_vma=False
    )
```

```python
import jax
import jax.numpy as jnp
from jax import lax
from jax.experimental import pallas as pl
from jax.experimental.pallas import tpu as pltpu
from jax.sharding import Mesh
from jax.sharding import PartitionSpec as P

DP = ("y", "xl", "z", "core")
SWAP = [(0, 1), (1, 0)]
F32 = jnp.float32
BF16 = jnp.bfloat16
SMEM = pl.BlockSpec(memory_space=pltpu.SMEM)
TILE = 512
LATE = 8


def cost(flops, *arrays, weight=1):
    moved = sum(4 * a.size for a in arrays)
    return pl.CostEstimate(
        flops=weight * flops, bytes_accessed=weight * moved, transcendentals=0
    )


def params():
    return pltpu.CompilerParams(vmem_limit_bytes=56 * 1024 * 1024)


def after(value, *earlier):
    return lax.optimization_barrier((value, *earlier))[0]


def halves(a):
    high = a.astype(BF16)
    return high, (a - high.astype(F32)).astype(BF16)


def dot(left, right):
    return jnp.dot(left, right, preferred_element_type=F32)


def three_passes(left_high, left_low, right):
    high, low = halves(right)
    return dot(left_high, high) + dot(left_high, low) + dot(left_low, high)


def turn_kernel(core_ref, x_ref, a_ref, x_mine, a_mine, theirs):
    even = core_ref[0] == 0
    for n, (src, mine) in enumerate(((x_ref, x_mine), (a_ref, a_mine))):
        t = src[...].T
        for z in range(4):
            for k in range(2):
                at = z * 32 + k * 8
                e, o = t[at : at + 8], t[at + 16 : at + 24]
                mine[k, 0, z, 0] = jnp.where(even, e, o)
                theirs[n, k, 0, z, 0] = jnp.where(even, o, e)


def turned(core, x, a):
    tokens = x.shape[0]
    mine = jax.ShapeDtypeStruct((2, 4, 4, 2, 8, tokens), F32)
    mine_spec = pl.BlockSpec((2, 1, 4, 1, 8, tokens), lambda i: (0, i // 2, 0, i % 2, 0, 0))
    column = pl.BlockSpec((tokens, 128), lambda i: (0, i))
    x_mine, a_mine, theirs = pl.pallas_call(
        turn_kernel,
        grid=(8,),
        in_specs=[SMEM, column, column],
        out_specs=[
            mine_spec,
            mine_spec,
            pl.BlockSpec((2, 2, 1, 4, 1, 8, tokens), lambda i: (0, 0, i // 2, 0, i % 2, 0, 0)),
        ],
        out_shape=[mine, mine, jax.ShapeDtypeStruct((2, *mine.shape), F32)],
        cost_estimate=cost(0, x, a, x, a),
        compiler_params=params(),
    )(core, x, a)
    return (
        x_mine.reshape(2, 256, tokens),
        a_mine.reshape(2, 256, tokens),
        theirs.reshape(2, 2, 256, tokens),
    )


def grad_kernel(p_ref, x_ref, xr_ref, a_ref, ar_ref, g_ref, b_ref, ro_ref, bo_ref, out, high, low):
    is_first = p_ref[0] == 0

    @pl.when(pl.program_id(0) == 0)
    def _():
        opened = x_ref[...] + xr_ref[...]
        second = jnp.where(is_first, ar_ref[...], a_ref[...])
        last = jnp.where(is_first, a_ref[...], opened)
        for n, v in enumerate((opened - second, second, last)):
            at = slice(n * 256, n * 256 + 256)
            high[at], low[at] = halves(v)

    b = b_ref[...]
    r = g_ref[...] - jnp.where(is_first, 0.0, b)
    right = jnp.concatenate([r, ro_ref[...]], axis=0)
    right_b = jnp.concatenate([b, bo_ref[...]], axis=0)
    both = three_passes(high[:512], low[:512], right)
    shared = three_passes(high[512:], low[512:], right_b)
    part0 = both[:256] - jnp.where(is_first, shared, 0.0)
    part1 = both[256:] + shared
    out[:, 0] = part0.reshape(16, 16, part0.shape[1])
    out[:, 1] = part1.reshape(16, 16, part1.shape[1])


def grad_parts(party, x, x_got, a, a_got, g, b, r_other, b_other, weight):
    tokens, ff = g.shape
    left = pl.BlockSpec((256, 2 * tokens), lambda n: (0, 0))
    right = pl.BlockSpec((tokens, TILE), lambda n: (0, n))
    return pl.pallas_call(
        grad_kernel,
        grid=(ff // TILE,),
        in_specs=[SMEM] + [left] * 4 + [right] * 4,
        out_specs=pl.BlockSpec((16, 2, 16, TILE), lambda n: (0, 0, 0, n)),
        out_shape=jax.ShapeDtypeStruct((16, 2, 16, ff), F32),
        scratch_shapes=[pltpu.VMEM((768, 2 * tokens), BF16)] * 2,
        cost_estimate=cost(3 * 2 * 768 * 2 * tokens * ff, x, x_got, a, a_got, g, b, r_other, b_other, g, g, weight=weight),
        compiler_params=params(),
    )(party, x, x_got, a, a_got, g, b, r_other, b_other)


def store_split(value, high, low):
    for xl in range(2):
        cols = [value[:, (2 * y + xl) * 128 :][:, :128] for y in range(4)]
        high[:, xl * 512 : xl * 512 + 512], low[:, xl * 512 : xl * 512 + 512] = halves(
            jnp.concatenate(cols, axis=1)
        )


def add_product(c_ref, w0_ref, w1_ref, out, high, low):
    w = jnp.concatenate([w0_ref[...], w1_ref[...]], axis=0)
    out[...] = c_ref[...] + three_passes(high[...], low[...], w)


def local_kernel(a_ref, w0_ref, w1_ref, c_ref, out, high, low):
    @pl.when(pl.program_id(0) == 0)
    def _():
        store_split(a_ref[...], high, low)

    add_product(c_ref, w0_ref, w1_ref, out, high, low)


def opened_kernel(x_ref, a_ref, got_ref, w0_ref, w1_ref, c_ref, out, high, low):
    @pl.when(pl.program_id(0) == 0)
    def _():
        store_split((x_ref[...] - a_ref[...]) + got_ref[...], high, low)

    add_product(c_ref, w0_ref, w1_ref, out, high, low)


def forward_call(kernel, lefts, left_rows, weights, at, c, row, rows):
    ff = c.shape[1]
    d = lefts[0].shape[1]
    steps = ff // TILE
    out_spec = pl.BlockSpec((rows, TILE), lambda n: (row, n))
    return pl.pallas_call(
        kernel,
        grid=(steps,),
        in_specs=[pl.BlockSpec((rows, d), lambda n, r=r: (r, 0)) for r in left_rows]
        + [
            pl.BlockSpec((d // 2, TILE), lambda n: (0, at * steps + n)),
            pl.BlockSpec((d // 2, TILE), lambda n: (0, (at + 2) * steps + n)),
            out_spec,
        ],
        out_specs=out_spec,
        out_shape=jax.ShapeDtypeStruct(c.shape, F32),
        scratch_shapes=[pltpu.VMEM((rows, d), BF16)] * 2,
        cost_estimate=cost(3 * 2 * rows * d * ff, weights, c),
        input_output_aliases={len(lefts) + 2: 0} if rows != c.shape[0] else {},
        compiler_params=params(),
    )(*lefts, weights, weights, c)


def scattered(a, axis, dim, *earlier):
    here = lax.axis_index(axis)
    total = lax.dynamic_index_in_dim(a, here, dim, keepdims=False)
    got = []
    for step in (2, 1, 3):
        piece = lax.dynamic_index_in_dim(a, (here + step) % 4, dim, keepdims=False)
        if earlier:
            piece = after(piece, *earlier)
        got.append(lax.ppermute(piece, axis, [(i, (i + step) % 4) for i in range(4)]))
    return total + got[0] + got[1] + got[2]


def body(x_share, w_share, g_share, fwd_a, fwd_b, fwd_c, bwd_a, bwd_b, bwd_c):
    x, w, g = x_share[0], w_share[0], g_share[0]
    fa, fb, fc = fwd_a[0], fwd_b[0], fwd_c[0]
    ba, bb, bc = bwd_a[0], bwd_b[0], bwd_c[0]
    party = lax.axis_index("party")
    party0 = party == 0
    first = party0.astype(F32)
    party_id = party.astype(jnp.int32).reshape(1)
    core_id = lax.axis_index("core").astype(jnp.int32).reshape(1)
    xl0 = lax.axis_index("xl") == 0
    ff = w.shape[1]

    d = w - fb
    d_party = lax.ppermute(d, "party", SWAP)
    near = lax.ppermute(jnp.concatenate([fb, d], axis=1), "xl", SWAP)
    d_across = lax.ppermute(d, ("party", "xl"), [(0, 3), (3, 0), (1, 2), (2, 1)])
    delta = d + d_party
    delta_near = near[:, ff:] + d_across
    packed = jnp.concatenate([fb + first * delta, delta], axis=1)
    packed_near = jnp.concatenate([near[:, :ff] + first * delta_near, delta_near], axis=1)
    weights = jnp.concatenate(
        [jnp.where(xl0, packed, packed_near), jnp.where(xl0, packed_near, packed)], axis=1
    )
    weights = lax.all_gather(weights, ("y", "z", "core"), axis=0, tiled=True)

    x_mine, a_mine, theirs = turned(core_id, x, ba)
    other = lax.ppermute(after(theirs, d_across, d_party, near), "core", SWAP)
    xs = [jnp.concatenate([x_mine[k], other[0, k]], axis=1) for k in range(2)]
    aa = [jnp.concatenate([a_mine[k], other[1, k]], axis=1) for k in range(2)]
    x0 = lax.ppermute(xs[0], "party", SWAP)
    a0 = lax.ppermute(aa[0], "party", [(1, 0)])
    x1 = lax.ppermute(xs[1], "party", SWAP)
    a1 = lax.ppermute(after(aa[1], x0), "party", [(1, 0)])
    u = x - fa
    u0 = lax.ppermute(after(u[:128], a0), "party", SWAP)
    u1 = lax.ppermute(after(u[128:256], x1), "party", SWAP)
    u2 = lax.ppermute(after(u[256:], a1), "party", SWAP)

    r_other = lax.ppermute(after(g - (1.0 - first) * bb, other), "core", SWAP)
    b_other = lax.ppermute(after(bb, other), "core", SWAP)
    rights = (g, bb, r_other, b_other)
    early = grad_parts(party_id, xs[0], x0, aa[0], a0, *rights, 1)
    late = grad_parts(party_id, xs[1], x1, aa[1], a1, *rights, LATE)

    early = lax.psum_scatter(early.reshape(16, 32, ff), ("y", "z"), scatter_dimension=0, tiled=True)
    early = early.reshape(2, 2, 8, ff)
    outputs = forward_call(local_kernel, (fa,), (0,), weights, 1, fc, 0, fc.shape[0])
    late = after(late, outputs, u0).reshape(4, 4, 2, 16, ff)
    part0 = scattered(late[:, :, 0], "z", 1)
    part1 = scattered(late[:, :, 1], "y", 0)
    part0 = scattered(part0, "y", 0, u1)
    part1 = scattered(part1, "z", 0, u1)
    late = jnp.stack([part0, part1]).reshape(2, 2, 8, ff)
    both = jnp.concatenate([early, late], axis=2)
    keep = jnp.where(xl0, both[:, 0], both[:, 1])
    give = jnp.where(xl0, both[:, 1], both[:, 0])
    both = keep + lax.ppermute(after(give, u2), "xl", SWAP)
    give = jnp.where(party0, both[1] - bc, both[0])
    keep = jnp.where(party0, both[0] + bc, both[1])
    grad = keep + lax.ppermute(give, "party", SWAP)

    outputs = forward_call(opened_kernel, (x, fa, u0), (0, 0, 0), weights, 0, outputs, 0, 128)
    outputs = forward_call(opened_kernel, (x, fa, u1), (1, 1, 0), weights, 0, outputs, 1, 128)
    outputs = forward_call(opened_kernel, (x, fa, u2), (1, 1, 0), weights, 0, outputs, 1, 256)
    return (outputs[None], grad[None])


def solution(mesh):
    split = Mesh(
        mesh.devices.reshape(mesh.shape["party"], 4, 2, 4, 2),
        ("party", *DP),
    )
    spec = P("party", DP, None)
    return jax.shard_map(
        body, mesh=split, in_specs=(spec,) * 9, out_specs=(spec, spec), check_vma=False
    )
```

```python
import jax
import jax.numpy as jnp
from jax import lax
from jax.experimental import pallas as pl
from jax.experimental.pallas import tpu as pltpu
from jax.sharding import Mesh
from jax.sharding import PartitionSpec as P

DP = ("y", "xl", "z", "core")
SWAP = [(0, 1), (1, 0)]
F32 = jnp.float32
BF16 = jnp.bfloat16
SMEM = pl.BlockSpec(memory_space=pltpu.SMEM)
TILE = 512
LATE = 8


def cost(flops, *arrays, weight=1):
    moved = sum(4 * a.size for a in arrays)
    return pl.CostEstimate(
        flops=weight * flops, bytes_accessed=weight * moved, transcendentals=0
    )


def params():
    return pltpu.CompilerParams(vmem_limit_bytes=56 * 1024 * 1024)


def after(value, *earlier):
    return lax.optimization_barrier((value, *earlier))[0]


def halves(a):
    high = a.astype(BF16)
    return high, (a - high.astype(F32)).astype(BF16)


def dot(left, right):
    return jnp.dot(left, right, preferred_element_type=F32)


def three_passes(left_high, left_low, right):
    high, low = halves(right)
    return dot(left_high, high) + dot(left_high, low) + dot(left_low, high)


def turn_kernel(core_ref, src, mine0, mine1, theirs):
    even = core_ref[0] == 0
    t = src[...].T
    for z in range(4):
        for k, mine in enumerate((mine0, mine1)):
            at = z * 32 + k * 8
            e, o = t[at : at + 8], t[at + 16 : at + 24]
            mine[0, z, 0] = jnp.where(even, e, o)
            theirs[k, 0, z, 0] = jnp.where(even, o, e)


def turned(core, share):
    tokens = share.shape[0]
    mine = jax.ShapeDtypeStruct((4, 4, 2, 8, tokens), F32)
    mine_spec = pl.BlockSpec((1, 4, 1, 8, tokens), lambda i: (i // 2, 0, i % 2, 0, 0))
    theirs_spec = pl.BlockSpec((2, 1, 4, 1, 8, tokens), lambda i: (0, i // 2, 0, i % 2, 0, 0))
    mine0, mine1, theirs = pl.pallas_call(
        turn_kernel,
        grid=(8,),
        in_specs=[SMEM, pl.BlockSpec((tokens, 128), lambda i: (0, i))],
        out_specs=[mine_spec, mine_spec, theirs_spec],
        out_shape=[mine, mine, jax.ShapeDtypeStruct((2, *mine.shape), F32)],
        cost_estimate=cost(0, share, share),
        compiler_params=params(),
    )(core, share)
    rows = 128 * 2
    return mine0.reshape(rows, tokens), mine1.reshape(rows, tokens), theirs.reshape(2, rows, tokens)


def right_of(is_first, g_ref, b_ref, go_ref, bo_ref, sent_refs):
    b, bo = b_ref[...], bo_ref[...]
    right = [g_ref[...] - jnp.where(is_first, 0.0, b), go_ref[...] - jnp.where(is_first, 0.0, bo)]
    right += [jnp.where(is_first, 0.0, ref[...]) for ref in sent_refs]
    return jnp.concatenate(right, axis=0), jnp.concatenate([b, bo], axis=0)


def x_kernel(split, p_ref, x_ref, a_ref, *refs):
    out, high, low = refs[-3:]
    got_refs, refs = (refs[:1], refs[1:]) if split else (refs[:2], refs[2:])
    width = x_ref.shape[1]
    is_first = p_ref[0] == 0

    @pl.when(pl.program_id(0) == 0)
    def _():
        x, got = x_ref[...], jnp.concatenate([ref[...] for ref in got_refs], axis=1)
        if split:
            col = lax.broadcasted_iota(jnp.int32, x.shape, 1)
            kept = jnp.logical_or(jnp.logical_not(is_first), col % 512 < 384)
            got = jnp.where(kept, got, 0.0)
        opened = x + got
        high[256:, :width], low[256:, :width] = halves(jnp.where(is_first, a_ref[...], opened))
        if split:
            opened = jnp.concatenate([opened, x[:, 384:512], x[:, 896:]], axis=1)
        high[:256], low[:256] = halves(opened)

    right, right_b = right_of(is_first, *refs[:4], refs[4:-3])
    shared = three_passes(high[256:, :width], low[256:, :width], right_b)
    out[0] = three_passes(high[:256], low[:256], right) - jnp.where(is_first, shared, 0.0)
    out[1] = shared


def a_kernel(split, p_ref, a_ref, early_ref, late_ref, s_ref, *refs):
    out, high, low = refs[-3:]
    is_first = p_ref[0] == 0

    @pl.when(pl.program_id(0) == 0)
    def _():
        a = a_ref[...]
        if split:
            zero = jnp.zeros((256, 128), F32)
            early, late = early_ref[...], late_ref[...]
            got = [early[:, 384:512], late[:, :256], zero, early[:, 896:], late[:, 256:], zero]
            second = jnp.where(is_first, jnp.concatenate(got, axis=1), a)
            second = jnp.concatenate([second, a[:, 384:512], a[:, 896:]], axis=1)
        else:
            second = jnp.where(is_first, late_ref[...], a)
        high[...], low[...] = halves(second)

    right, _ = right_of(is_first, *refs[:4], refs[4:-3])
    product = three_passes(high[...], low[...], right)
    out[:, 0] = (s_ref[0] - product).reshape(16, 16, product.shape[1])
    out[:, 1] = (s_ref[1] + product).reshape(16, 16, product.shape[1])


def right_specs(tokens, sent):
    right = pl.BlockSpec((tokens, TILE), lambda n: (0, n))
    per = sent[0].shape[1] // TILE if sent else 1
    part = pl.BlockSpec((128, TILE), lambda n: (n // per, n % per))
    return [right] * 4 + [part] * len(sent)


def x_parts(party, x, x_got, a, rights, sent, weight):
    tokens, ff = rights[0].shape
    left = pl.BlockSpec((256, 2 * tokens), lambda n: (0, 0))
    depth = 2 * tokens + 128 * len(sent)
    return pl.pallas_call(
        lambda *refs: x_kernel(bool(sent), *refs),
        grid=(ff // TILE,),
        in_specs=[SMEM, left, left]
        + [pl.BlockSpec(v.shape, lambda n: (0, 0)) for v in x_got]
        + right_specs(tokens, sent),
        out_specs=pl.BlockSpec((2, 256, TILE), lambda n: (0, 0, n)),
        out_shape=jax.ShapeDtypeStruct((2, 256, ff), F32),
        scratch_shapes=[pltpu.VMEM((512, depth), BF16)] * 2,
        cost_estimate=cost(3 * 2 * 512 * depth * ff, *rights, x, x, weight=weight),
        compiler_params=params(),
    )(party, x, a, *x_got, *rights, *sent)


def a_parts(party, a, early, late, s, rights, sent, weight):
    tokens, ff = rights[0].shape
    lefts = [pl.BlockSpec(v.shape, lambda n: (0, 0)) for v in (a, early, late)]
    depth = 2 * tokens + 128 * len(sent)
    return pl.pallas_call(
        lambda *refs: a_kernel(bool(sent), *refs),
        grid=(ff // TILE,),
        in_specs=[SMEM, *lefts, pl.BlockSpec((2, 256, TILE), lambda n: (0, 0, n))]
        + right_specs(tokens, sent),
        out_specs=pl.BlockSpec((16, 2, 16, TILE), lambda n: (0, 0, 0, n)),
        out_shape=jax.ShapeDtypeStruct((16, 2, 16, ff), F32),
        scratch_shapes=[pltpu.VMEM((256, depth), BF16)] * 2,
        cost_estimate=cost(3 * 2 * 256 * depth * ff, *rights, s, s, weight=weight),
        compiler_params=params(),
    )(party, a, early, late, s, *rights, *sent)


def store_split(value, high, low):
    for xl in range(2):
        cols = [value[:, (2 * y + xl) * 128 :][:, :128] for y in range(4)]
        high[:, xl * 512 : xl * 512 + 512], low[:, xl * 512 : xl * 512 + 512] = halves(
            jnp.concatenate(cols, axis=1)
        )


def add_product(c_ref, w0_ref, w1_ref, out, high, low):
    w = jnp.concatenate([w0_ref[...], w1_ref[...]], axis=0)
    out[...] = c_ref[...] + three_passes(high[...], low[...], w)


def local_kernel(a_ref, w0_ref, w1_ref, c_ref, out, high, low):
    @pl.when(pl.program_id(0) == 0)
    def _():
        store_split(a_ref[...], high, low)

    add_product(c_ref, w0_ref, w1_ref, out, high, low)


def opened_kernel(x_ref, a_ref, got_ref, w0_ref, w1_ref, c_ref, out, high, low):
    @pl.when(pl.program_id(0) == 0)
    def _():
        store_split((x_ref[...] - a_ref[...]) + got_ref[...], high, low)

    add_product(c_ref, w0_ref, w1_ref, out, high, low)


def forward_call(kernel, lefts, left_rows, weights, at, c, row, rows):
    ff = c.shape[1]
    d = lefts[0].shape[1]
    steps = ff // TILE
    out_spec = pl.BlockSpec((rows, TILE), lambda n: (row, n))
    return pl.pallas_call(
        kernel,
        grid=(steps,),
        in_specs=[pl.BlockSpec((rows, d), lambda n, r=r: (r, 0)) for r in left_rows]
        + [
            pl.BlockSpec((d // 2, TILE), lambda n: (0, at * steps + n)),
            pl.BlockSpec((d // 2, TILE), lambda n: (0, (at + 2) * steps + n)),
            out_spec,
        ],
        out_specs=out_spec,
        out_shape=jax.ShapeDtypeStruct(c.shape, F32),
        scratch_shapes=[pltpu.VMEM((rows, d), BF16)] * 2,
        cost_estimate=cost(3 * 2 * rows * d * ff, weights, c),
        input_output_aliases={len(lefts) + 2: 0} if rows != c.shape[0] else {},
        compiler_params=params(),
    )(*lefts, weights, weights, c)


def scattered_pair(a, a_axis, a_dim, b, b_axis, b_dim, first=(), last=()):
    sums, got = [], [[], []]
    for v, axis, dim in ((a, a_axis, a_dim), (b, b_axis, b_dim)):
        here = lax.axis_index(axis)
        sums.append(lax.dynamic_index_in_dim(v, here, dim, keepdims=False))
    for step in (2, 1, 3):
        for n, (v, axis, dim) in enumerate(((a, a_axis, a_dim), (b, b_axis, b_dim))):
            here = lax.axis_index(axis)
            piece = lax.dynamic_index_in_dim(v, (here + step) % 4, dim, keepdims=False)
            if len(got[n]) < 2:
                piece = after(piece, *first)
            else:
                piece = after(piece, got[n][0], *last)
            got[n].append(lax.ppermute(piece, axis, [(i, (i + step) % 4) for i in range(4)]))
    return [s + r[0] + r[1] + r[2] for s, r in zip(sums, got)]


def body(x_share, w_share, g_share, fwd_a, fwd_b, fwd_c, bwd_a, bwd_b, bwd_c):
    x, w, g = x_share[0], w_share[0], g_share[0]
    fa, fb, fc = fwd_a[0], fwd_b[0], fwd_c[0]
    ba, bb, bc = bwd_a[0], bwd_b[0], bwd_c[0]
    party = lax.axis_index("party")
    party0 = party == 0
    first = party0.astype(F32)
    party_id = party.astype(jnp.int32).reshape(1)
    core_id = lax.axis_index("core").astype(jnp.int32).reshape(1)
    xl0 = lax.axis_index("xl") == 0
    ff = w.shape[1]

    x_mine0, x_mine1, x_theirs = turned(core_id, x)
    x0 = lax.ppermute(x_mine0, "party", SWAP)
    x_other = lax.ppermute(x_theirs, "core", SWAP)
    xs0 = jnp.concatenate([x_mine0, x_other[0]], axis=1)
    xs1 = jnp.concatenate([x_mine1, x_other[1]], axis=1)
    x0_other = lax.ppermute(x_other[0], "party", SWAP)
    a_mine0, a_mine1, a_theirs = turned(core_id, after(ba, x_theirs))
    a_other = lax.ppermute(a_theirs, "core", SWAP)
    aa0 = jnp.concatenate([a_mine0, a_other[0]], axis=1)
    aa1 = jnp.concatenate([a_mine1, a_other[1]], axis=1)
    d = after(w - fb, a_theirs)
    d_party = lax.ppermute(d, "party", SWAP)
    near = lax.ppermute(jnp.concatenate([fb, d], axis=1), "xl", SWAP)
    d_across = lax.ppermute(d, ("party", "xl"), [(0, 3), (3, 0), (1, 2), (2, 1)])
    delta = d + d_party
    delta_near = near[:, ff:] + d_across
    packed = jnp.concatenate([fb + first * delta, delta], axis=1)
    packed_near = jnp.concatenate([near[:, :ff] + first * delta_near, delta_near], axis=1)
    weights = jnp.concatenate(
        [jnp.where(xl0, packed, packed_near), jnp.where(xl0, packed_near, packed)], axis=1
    )
    weights = lax.all_gather(after(weights, x0, x_other, a_other), ("y", "z", "core"), axis=0, tiled=True)

    last = g[3 * g.shape[0] // 4 :]
    last = jnp.concatenate([last[:, : ff // 2], last[:, ff // 2 :]], axis=0)
    a0_sent = jnp.where(party0, last, aa0)
    a0 = lax.ppermute(a0_sent, "party", SWAP)
    x1_sent = jnp.concatenate(
        [
            xs1[:, :384],
            jnp.where(party0, xs1[:, 384:512], aa1[:, :128]),
            xs1[:, 512:896],
            jnp.where(party0, xs1[:, 896:], aa1[:, 512:640]),
        ],
        axis=1,
    )
    x1 = lax.ppermute(x1_sent, "party", SWAP)
    a1 = jnp.concatenate([aa1[:, 128:384], aa1[:, 640:896]], axis=1)
    a1 = lax.ppermute(after(a1, x0_other), "party", [(1, 0)])
    u = x - fa
    half = x.shape[0] // 2
    u0 = lax.ppermute(after(u[: half // 2], a0), "party", SWAP)
    u1 = lax.ppermute(after(u[half // 2 : half], x1), "party", SWAP)
    u2 = lax.ppermute(after(u[half:], x1), "party", SWAP)

    g_other = lax.ppermute(after(g, x0, a0_sent), "core", SWAP)
    b_other = lax.ppermute(after(bb, x0, x1_sent), "core", SWAP)
    rights = (g, bb, g_other, b_other)
    early = x_parts(party_id, xs0, (x0, x0_other), aa0, rights, (), 1)
    sent = (a0, lax.ppermute(after(a0, early), "core", SWAP))
    early = a_parts(party_id, aa0, a0, a0, early, rights, (), 1)
    late = x_parts(party_id, xs1, (x1,), aa1, rights, sent, LATE)
    late = a_parts(party_id, aa1, x1, a1, late, rights, sent, LATE)

    early = lax.psum_scatter(early.reshape(16, 32, ff), ("y", "z"), scatter_dimension=0, tiled=True)
    early = early.reshape(2, 2, 8, ff)
    outputs = forward_call(local_kernel, (fa,), (0,), weights, 1, fc, 0, fc.shape[0])
    late = after(late, outputs).reshape(4, 4, 2, 16, ff)
    part0, part1 = scattered_pair(late[:, :, 0], "z", 1, late[:, :, 1], "y", 0, (), (u0,))
    part0, part1 = scattered_pair(part0, "y", 0, part1, "z", 0, (u1,))
    late = jnp.stack([part0, part1]).reshape(2, 2, 8, ff)
    both = jnp.concatenate([early, late], axis=2)
    keep = jnp.where(xl0, both[:, 0], both[:, 1])
    give = jnp.where(xl0, both[:, 1], both[:, 0])
    both = keep + lax.ppermute(after(give, u2), "xl", SWAP)
    give = jnp.where(party0, both[1] - bc, both[0])
    keep = jnp.where(party0, both[0] + bc, both[1])
    grad = keep + lax.ppermute(give, "party", SWAP)

    outputs = forward_call(opened_kernel, (x, fa, jnp.concatenate([u0, u1])), (0, 0, 0), weights, 0, outputs, 0, half)
    outputs = forward_call(opened_kernel, (x, fa, u2), (1, 1, 0), weights, 0, outputs, 1, half)
    return (outputs[None], grad[None])


def solution(mesh):
    split = Mesh(
        mesh.devices.reshape(mesh.shape["party"], 4, 2, 4, 2),
        ("party", *DP),
    )
    spec = P("party", DP, None)
    return jax.shard_map(
        body, mesh=split, in_specs=(spec,) * 9, out_specs=(spec, spec), check_vma=False
    )
```

```python
import jax
import jax.numpy as jnp
from jax import lax
from jax.experimental import pallas as pl
from jax.experimental.pallas import tpu as pltpu
from jax.sharding import Mesh
from jax.sharding import PartitionSpec as P

DP = ("y", "xl", "z", "core")
SWAP = [(0, 1), (1, 0)]
F32 = jnp.float32
BF16 = jnp.bfloat16
SMEM = pl.BlockSpec(memory_space=pltpu.SMEM)
TILE = 512
LATE = 8


def cost(flops, *arrays, weight=1):
    moved = sum(4 * a.size for a in arrays)
    return pl.CostEstimate(
        flops=weight * flops, bytes_accessed=weight * moved, transcendentals=0
    )


def params():
    return pltpu.CompilerParams(vmem_limit_bytes=56 * 1024 * 1024)


def after(value, *earlier):
    return lax.optimization_barrier((value, *earlier))[0]


def halves(a):
    high = a.astype(BF16)
    return high, (a - high.astype(F32)).astype(BF16)


def dot(left, right):
    return jnp.dot(left, right, preferred_element_type=F32)


def three_passes(left_high, left_low, right):
    high, low = halves(right)
    return dot(left_high, high) + dot(left_high, low) + dot(left_low, high)


def turn_kernel(core_ref, src, mine0, mine1, theirs):
    even = core_ref[0] == 0
    t = src[...].T
    for z in range(4):
        for k, mine in enumerate((mine0, mine1)):
            at = z * 32 + k * 8
            e, o = t[at : at + 8], t[at + 16 : at + 24]
            mine[0, z, 0] = jnp.where(even, e, o)
            theirs[k, 0, z, 0] = jnp.where(even, o, e)


def turned(core, share):
    tokens = share.shape[0]
    mine = jax.ShapeDtypeStruct((4, 4, 2, 8, tokens), F32)
    mine_spec = pl.BlockSpec((1, 4, 1, 8, tokens), lambda i: (i // 2, 0, i % 2, 0, 0))
    theirs_spec = pl.BlockSpec((2, 1, 4, 1, 8, tokens), lambda i: (0, i // 2, 0, i % 2, 0, 0))
    mine0, mine1, theirs = pl.pallas_call(
        turn_kernel,
        grid=(8,),
        in_specs=[SMEM, pl.BlockSpec((tokens, 128), lambda i: (0, i))],
        out_specs=[mine_spec, mine_spec, theirs_spec],
        out_shape=[mine, mine, jax.ShapeDtypeStruct((2, *mine.shape), F32)],
        cost_estimate=cost(0, share, share),
        compiler_params=params(),
    )(core, share)
    rows = 128 * 2
    return mine0.reshape(rows, tokens), mine1.reshape(rows, tokens), theirs.reshape(2, rows, tokens)


def passes(left_high, left_low, high, low):
    return dot(left_high, high) + dot(left_high, low) + dot(left_low, high)


def split_kernel(p_ref, g_ref, b_ref, go_ref, bo_ref, r_high, r_low, b_high, b_low):
    own = pl.program_id(0) < pl.num_programs(0) // 2
    b = jnp.where(own, b_ref[...], bo_ref[...])
    r = jnp.where(own, g_ref[...], go_ref[...]) - jnp.where(p_ref[0] == 0, 0.0, b)
    r_high[...], r_low[...] = halves(r)
    b_high[...], b_low[...] = halves(b)


def split_rights(party, g, b, g_other, b_other):
    tokens, ff = g.shape
    block, steps = 128, tokens // 128
    mine = pl.BlockSpec((block, ff), lambda i: (jnp.minimum(i, steps - 1), 0))
    other = pl.BlockSpec((block, ff), lambda i: (jnp.maximum(i - steps, 0), 0))
    out = jax.ShapeDtypeStruct((2 * tokens, ff), BF16)
    return pl.pallas_call(
        split_kernel,
        grid=(2 * steps,),
        in_specs=[SMEM, mine, mine, other, other],
        out_specs=[pl.BlockSpec((block, ff), lambda i: (i, 0))] * 4,
        out_shape=[out] * 4,
        cost_estimate=cost(0, g, g, g, g, g, g, g, g),
        compiler_params=params(),
    )(party, g, b, g_other, b_other)


def sent_of(is_first, refs):
    return halves(jnp.where(is_first, 0.0, jnp.concatenate([ref[...] for ref in refs], axis=0)))


def x_kernel(split, p_ref, x_ref, a_ref, *refs):
    out, high, low = refs[-3:]
    got_refs, refs = (refs[:1], refs[1:]) if split else (refs[:2], refs[2:])
    width = x_ref.shape[1]
    is_first = p_ref[0] == 0

    @pl.when(pl.program_id(0) == 0)
    def _():
        x, got = x_ref[...], jnp.concatenate([ref[...] for ref in got_refs], axis=1)
        if split:
            col = lax.broadcasted_iota(jnp.int32, x.shape, 1)
            kept = jnp.logical_or(jnp.logical_not(is_first), col % 512 < 384)
            got = jnp.where(kept, got, 0.0)
        opened = x + got
        high[256:, :width], low[256:, :width] = halves(jnp.where(is_first, a_ref[...], opened))
        if split:
            opened = jnp.concatenate([opened, x[:, 384:512], x[:, 896:]], axis=1)
        high[:256], low[:256] = halves(opened)

    r_high, r_low, b_high, b_low = refs[:4]
    shared = passes(high[256:, :width], low[256:, :width], b_high[...], b_low[...])
    product = passes(high[:256, :width], low[:256, :width], r_high[...], r_low[...])
    if split:
        product += passes(high[:256, width:], low[:256, width:], *sent_of(is_first, refs[4:-3]))
    out[0] = product - jnp.where(is_first, shared, 0.0)
    out[1] = shared


def a_kernel(split, p_ref, a_ref, early_ref, late_ref, s_ref, *refs):
    out, high, low = refs[-3:]
    is_first = p_ref[0] == 0

    @pl.when(pl.program_id(0) == 0)
    def _():
        a = a_ref[...]
        if split:
            zero = jnp.zeros((256, 128), F32)
            early, late = early_ref[...], late_ref[...]
            got = [early[:, 384:512], late[:, :256], zero, early[:, 896:], late[:, 256:], zero]
            second = jnp.where(is_first, jnp.concatenate(got, axis=1), a)
            second = jnp.concatenate([second, a[:, 384:512], a[:, 896:]], axis=1)
        else:
            second = jnp.where(is_first, late_ref[...], a)
        high[...], low[...] = halves(second)

    width = a_ref.shape[1]
    product = passes(high[:, :width], low[:, :width], refs[0][...], refs[1][...])
    if split:
        product += passes(high[:, width:], low[:, width:], *sent_of(is_first, refs[2:-3]))
    out[:, 0] = (s_ref[0] - product).reshape(16, 16, product.shape[1])
    out[:, 1] = (s_ref[1] + product).reshape(16, 16, product.shape[1])


def right_specs(rights, sent):
    per = sent[0].shape[1] // TILE if sent else 1
    part = pl.BlockSpec((128, TILE), lambda n: (n // per, n % per))
    return [pl.BlockSpec((v.shape[0], TILE), lambda n: (0, n)) for v in rights] + [part] * len(sent)


def x_parts(party, x, x_got, a, rights, sent, weight):
    tokens, ff = rights[0].shape
    left = pl.BlockSpec((256, tokens), lambda n: (0, 0))
    depth = tokens + 128 * len(sent)
    return pl.pallas_call(
        lambda *refs: x_kernel(bool(sent), *refs),
        grid=(ff // TILE,),
        in_specs=[SMEM, left, left]
        + [pl.BlockSpec(v.shape, lambda n: (0, 0)) for v in x_got]
        + right_specs(rights, sent),
        out_specs=pl.BlockSpec((2, 256, TILE), lambda n: (0, 0, n)),
        out_shape=jax.ShapeDtypeStruct((2, 256, ff), F32),
        scratch_shapes=[pltpu.VMEM((512, depth), BF16)] * 2,
        cost_estimate=cost(3 * 2 * 512 * depth * ff, *rights, x, x, weight=weight),
        compiler_params=params(),
    )(party, x, a, *x_got, *rights, *sent)


def a_parts(party, a, early, late, s, rights, sent, weight):
    tokens, ff = rights[0].shape
    lefts = [pl.BlockSpec(v.shape, lambda n: (0, 0)) for v in (a, early, late)]
    depth = tokens + 128 * len(sent)
    return pl.pallas_call(
        lambda *refs: a_kernel(bool(sent), *refs),
        grid=(ff // TILE,),
        in_specs=[SMEM, *lefts, pl.BlockSpec((2, 256, TILE), lambda n: (0, 0, n))]
        + right_specs(rights, sent),
        out_specs=pl.BlockSpec((16, 2, 16, TILE), lambda n: (0, 0, 0, n)),
        out_shape=jax.ShapeDtypeStruct((16, 2, 16, ff), F32),
        scratch_shapes=[pltpu.VMEM((256, depth), BF16)] * 2,
        cost_estimate=cost(3 * 2 * 256 * depth * ff, *rights, s, s, weight=weight),
        compiler_params=params(),
    )(party, a, early, late, s, *rights, *sent)


def store_split(value, high, low):
    for xl in range(2):
        cols = [value[:, (2 * y + xl) * 128 :][:, :128] for y in range(4)]
        high[:, xl * 512 : xl * 512 + 512], low[:, xl * 512 : xl * 512 + 512] = halves(
            jnp.concatenate(cols, axis=1)
        )


def add_product(c_ref, w0_ref, w1_ref, out, high, low):
    w = jnp.concatenate([w0_ref[...], w1_ref[...]], axis=0)
    out[...] = c_ref[...] + three_passes(high[...], low[...], w)


def local_kernel(a_ref, w0_ref, w1_ref, c_ref, out, high, low):
    @pl.when(pl.program_id(0) == 0)
    def _():
        store_split(a_ref[...], high, low)

    add_product(c_ref, w0_ref, w1_ref, out, high, low)


def opened_kernel(x_ref, a_ref, got_ref, w0_ref, w1_ref, c_ref, out, high, low):
    @pl.when(pl.program_id(0) == 0)
    def _():
        store_split((x_ref[...] - a_ref[...]) + got_ref[...], high, low)

    add_product(c_ref, w0_ref, w1_ref, out, high, low)


def forward_call(kernel, lefts, left_rows, weights, at, c, row, rows):
    ff = c.shape[1]
    d = lefts[0].shape[1]
    steps = ff // TILE
    out_spec = pl.BlockSpec((rows, TILE), lambda n: (row, n))
    return pl.pallas_call(
        kernel,
        grid=(steps,),
        in_specs=[pl.BlockSpec((rows, d), lambda n, r=r: (r, 0)) for r in left_rows]
        + [
            pl.BlockSpec((d // 2, TILE), lambda n: (0, at * steps + n)),
            pl.BlockSpec((d // 2, TILE), lambda n: (0, (at + 2) * steps + n)),
            out_spec,
        ],
        out_specs=out_spec,
        out_shape=jax.ShapeDtypeStruct(c.shape, F32),
        scratch_shapes=[pltpu.VMEM((rows, d), BF16)] * 2,
        cost_estimate=cost(3 * 2 * rows * d * ff, weights, c),
        input_output_aliases={len(lefts) + 2: 0} if rows != c.shape[0] else {},
        compiler_params=params(),
    )(*lefts, weights, weights, c)


def scattered_pair(a, a_axis, a_dim, b, b_axis, b_dim, first=(), last=()):
    sums, got = [], [[], []]
    for v, axis, dim in ((a, a_axis, a_dim), (b, b_axis, b_dim)):
        here = lax.axis_index(axis)
        sums.append(lax.dynamic_index_in_dim(v, here, dim, keepdims=False))
    for step in (2, 1, 3):
        for n, (v, axis, dim) in enumerate(((a, a_axis, a_dim), (b, b_axis, b_dim))):
            here = lax.axis_index(axis)
            piece = lax.dynamic_index_in_dim(v, (here + step) % 4, dim, keepdims=False)
            if len(got[n]) < 2:
                piece = after(piece, *first)
            else:
                piece = after(piece, got[n][0], *last)
            got[n].append(lax.ppermute(piece, axis, [(i, (i + step) % 4) for i in range(4)]))
    return [s + r[0] + r[1] + r[2] for s, r in zip(sums, got)]


def body(x_share, w_share, g_share, fwd_a, fwd_b, fwd_c, bwd_a, bwd_b, bwd_c):
    x, w, g = x_share[0], w_share[0], g_share[0]
    fa, fb, fc = fwd_a[0], fwd_b[0], fwd_c[0]
    ba, bb, bc = bwd_a[0], bwd_b[0], bwd_c[0]
    party = lax.axis_index("party")
    party0 = party == 0
    first = party0.astype(F32)
    party_id = party.astype(jnp.int32).reshape(1)
    core_id = lax.axis_index("core").astype(jnp.int32).reshape(1)
    xl0 = lax.axis_index("xl") == 0
    ff = w.shape[1]

    x_mine0, x_mine1, x_theirs = turned(core_id, x)
    x0 = lax.ppermute(x_mine0, "party", SWAP)
    x_other = lax.ppermute(x_theirs, "core", SWAP)
    xs0 = jnp.concatenate([x_mine0, x_other[0]], axis=1)
    xs1 = jnp.concatenate([x_mine1, x_other[1]], axis=1)
    x0_other = lax.ppermute(x_other[0], "party", SWAP)
    a_mine0, a_mine1, a_theirs = turned(core_id, after(ba, x_other))
    a_other = lax.ppermute(a_theirs, "core", SWAP)
    aa0 = jnp.concatenate([a_mine0, a_other[0]], axis=1)
    aa1 = jnp.concatenate([a_mine1, a_other[1]], axis=1)
    d = w - fb
    d_party = lax.ppermute(d, "party", SWAP)
    near = lax.ppermute(jnp.concatenate([fb, d], axis=1), "xl", SWAP)
    d_across = lax.ppermute(d, ("party", "xl"), [(0, 3), (3, 0), (1, 2), (2, 1)])
    d_party, near, d_across = lax.optimization_barrier((d_party, near, d_across, x_theirs))[:3]
    delta = d + d_party
    delta_near = near[:, ff:] + d_across
    packed = jnp.concatenate([fb + first * delta, delta], axis=1)
    packed_near = jnp.concatenate([near[:, :ff] + first * delta_near, delta_near], axis=1)
    weights = jnp.concatenate(
        [jnp.where(xl0, packed, packed_near), jnp.where(xl0, packed_near, packed)], axis=1
    )
    weights = lax.all_gather(after(weights, x0, x_other, a_other), ("y", "z", "core"), axis=0, tiled=True)

    last = g[3 * g.shape[0] // 4 :]
    last = jnp.concatenate([last[:, : ff // 2], last[:, ff // 2 :]], axis=0)
    a0_sent = jnp.where(party0, last, aa0)
    a0 = lax.ppermute(a0_sent, "party", SWAP)
    x1_sent = jnp.concatenate(
        [
            xs1[:, :384],
            jnp.where(party0, xs1[:, 384:512], aa1[:, :128]),
            xs1[:, 512:896],
            jnp.where(party0, xs1[:, 896:], aa1[:, 512:640]),
        ],
        axis=1,
    )
    x1 = lax.ppermute(x1_sent, "party", SWAP)
    a1 = jnp.concatenate([aa1[:, 128:384], aa1[:, 640:896]], axis=1)
    a1 = lax.ppermute(after(a1, x0_other), "party", [(1, 0)])
    u = x - fa
    half = x.shape[0] // 2
    u0 = lax.ppermute(after(u[:half], a0), "party", SWAP)
    u1 = lax.ppermute(after(u[half:], x1), "party", SWAP)

    g_other = lax.ppermute(after(g, a_theirs), "core", SWAP)
    b_other = lax.ppermute(after(bb, a_theirs), "core", SWAP)
    rights = split_rights(party_id, g, bb, g_other, b_other)
    early = x_parts(party_id, xs0, (x0, x0_other), aa0, rights, (), 1)
    sent = (a0, lax.ppermute(after(a0, early), "core", SWAP))
    early = a_parts(party_id, aa0, a0, a0, early, rights[:2], (), 1)
    late = x_parts(party_id, xs1, (x1,), aa1, rights, sent, LATE)
    late = a_parts(party_id, aa1, x1, a1, late, rights[:2], sent, LATE)

    early = lax.psum_scatter(early.reshape(16, 32, ff), ("y", "z"), scatter_dimension=0, tiled=True)
    early = early.reshape(2, 2, 8, ff)
    outputs = forward_call(local_kernel, (fa,), (0,), weights, 1, fc, 0, fc.shape[0])
    late = late.reshape(4, 4, 2, 16, ff)
    part0, part1 = scattered_pair(late[:, :, 0], "z", 1, late[:, :, 1], "y", 0, (), (u0,))
    part0, part1 = scattered_pair(part0, "y", 0, part1, "z", 0, (outputs,))
    late = jnp.stack([part0, part1]).reshape(2, 2, 8, ff)
    both = jnp.concatenate([early, late], axis=2)
    keep = jnp.where(xl0, both[:, 0], both[:, 1])
    give = jnp.where(xl0, both[:, 1], both[:, 0])
    both = keep + lax.ppermute(after(give, u1), "xl", SWAP)
    give = jnp.where(party0, both[1] - bc, both[0])
    keep = jnp.where(party0, both[0] + bc, both[1])
    grad = keep + lax.ppermute(give, "party", SWAP)

    outputs = forward_call(opened_kernel, (x, fa, u0), (0, 0, 0), weights, 0, outputs, 0, half)
    outputs = forward_call(opened_kernel, (x, fa, u1), (1, 1, 0), weights, 0, outputs, 1, half)
    return (outputs[None], grad[None])


def solution(mesh):
    split = Mesh(
        mesh.devices.reshape(mesh.shape["party"], 4, 2, 4, 2),
        ("party", *DP),
    )
    spec = P("party", DP, None)
    return jax.shard_map(
        body, mesh=split, in_specs=(spec,) * 9, out_specs=(spec, spec), check_vma=False
    )
```

```python
import jax
import jax.numpy as jnp
from jax import lax
from jax.experimental import pallas as pl
from jax.experimental.pallas import tpu as pltpu
from jax.sharding import Mesh
from jax.sharding import PartitionSpec as P

DP = ("y", "xl", "z", "core")
SWAP = [(0, 1), (1, 0)]
F32 = jnp.float32
BF16 = jnp.bfloat16
SMEM = pl.BlockSpec(memory_space=pltpu.SMEM)
TILE = 512
LATE = 8


def cost(flops, *arrays, weight=1):
    moved = sum(4 * a.size for a in arrays)
    return pl.CostEstimate(
        flops=weight * flops, bytes_accessed=weight * moved, transcendentals=0
    )


def params():
    return pltpu.CompilerParams(vmem_limit_bytes=56 * 1024 * 1024)


def after(value, *earlier):
    return lax.optimization_barrier((value, *earlier))[0]


def halves(a):
    high = a.astype(BF16)
    return high, (a - high.astype(F32)).astype(BF16)


def dot(left, right):
    return jnp.dot(left, right, preferred_element_type=F32)


def turn_kernel(core_ref, src, mine0, mine1, theirs):
    even = core_ref[0] == 0
    t = src[...].T
    for y in range(mine0.shape[1]):
        for xl in range(2):
            for z in range(4):
                for k, mine in enumerate((mine0, mine1)):
                    at = (2 * y + xl) * 128 + z * 32 + k * 8
                    e, o = t[at : at + 8], t[at + 16 : at + 24]
                    mine[z, y, xl] = jnp.where(even, e, o)
                    theirs[k, z, y, xl] = jnp.where(even, o, e)


def turned(core, share):
    tokens = share.shape[0]
    mine = jax.ShapeDtypeStruct((4, 4, 2, 8, tokens), F32)
    mine_spec = pl.BlockSpec((4, 2, 2, 8, tokens), lambda i: (0, i, 0, 0, 0))
    theirs_spec = pl.BlockSpec((2, 4, 2, 2, 8, tokens), lambda i: (0, 0, i, 0, 0, 0))
    mine0, mine1, theirs = pl.pallas_call(
        turn_kernel,
        grid=(2,),
        in_specs=[SMEM, pl.BlockSpec((tokens, 512), lambda i: (0, i))],
        out_specs=[mine_spec, mine_spec, theirs_spec],
        out_shape=[mine, mine, jax.ShapeDtypeStruct((2, *mine.shape), F32)],
        cost_estimate=cost(0, share, share),
        compiler_params=params(),
    )(core, share)
    rows = 128 * 2
    return mine0.reshape(rows, tokens), mine1.reshape(rows, tokens), theirs.reshape(2, rows, tokens)


def passes(stack, right):
    rows = stack.shape[0] // 2
    high, low = halves(right)
    both = dot(stack[...], high)
    return both[:rows] + both[rows:] + dot(stack[:rows], low)


def grad_kernel(split, p_ref, x_ref, a_ref, *refs):
    out, pair, pair_sent, single = refs[-4:]
    got_refs, refs = (refs[:1], refs[1:]) if split else (refs[:2], refs[2:])
    g_ref, b_ref, go_ref, bo_ref = refs[:4]
    sent_refs = refs[4:-4]
    is_first = p_ref[0] == 0

    @pl.when(pl.program_id(0) == 0)
    def _():
        x, a = x_ref[...], a_ref[...]
        if split:
            got, late = got_refs[0][:, :1024], got_refs[0][:, 1024:]
            col = lax.broadcasted_iota(jnp.int32, x.shape, 1)
            kept = jnp.logical_or(jnp.logical_not(is_first), col % 512 < 384)
            zero = jnp.zeros((256, 128), F32)
            second = [got[:, 384:512], late[:, :256], zero, got[:, 896:], late[:, 256:], zero]
            second = jnp.where(is_first, jnp.concatenate(second, axis=1), a)
            got = jnp.where(kept, got, 0.0)
            a_sent = jnp.concatenate([a[:, 384:512], a[:, 896:]], axis=1)
            x_sent = jnp.concatenate([x[:, 384:512], x[:, 896:]], axis=1)
            pair_sent[:256], pair_sent[512:768] = halves(x_sent - a_sent)
            pair_sent[256:512], pair_sent[768:] = halves(a_sent)
        else:
            got = jnp.concatenate([got_refs[0][...], got_refs[1][:, :512]], axis=1)
            second = jnp.where(is_first, got_refs[1][:, 512:], a)
        opened = x + got
        pair[:256], pair[512:768] = halves(opened - second)
        pair[256:512], pair[768:] = halves(second)
        single[:256], single[256:] = halves(jnp.where(is_first, a, opened))

    b, bo = b_ref[...], bo_ref[...]
    r = g_ref[...] - jnp.where(is_first, 0.0, b)
    ro = go_ref[...] - jnp.where(is_first, 0.0, bo)
    both = passes(pair, jnp.concatenate([r, ro], axis=0))
    if split:
        sent = jnp.concatenate([ref[...] for ref in sent_refs], axis=0)
        both += passes(pair_sent, jnp.where(is_first, 0.0, sent))
    shared = passes(single, jnp.concatenate([b, bo], axis=0))
    part0 = both[:256] - jnp.where(is_first, shared, 0.0)
    part1 = both[256:] + shared
    out[:, 0] = part0.reshape(16, 16, part0.shape[1])
    out[:, 1] = part1.reshape(16, 16, part1.shape[1])


def grad_parts(party, x, a, got, rights, sent, weight):
    tokens, ff = rights[0].shape
    lefts = (x, a, *got)
    right = pl.BlockSpec((tokens, TILE), lambda n: (0, n))
    skip, per = 512 // TILE, 1024 // TILE
    part = pl.BlockSpec((128, TILE), lambda n: (n // per, skip + n % per))
    return pl.pallas_call(
        lambda *refs: grad_kernel(bool(sent), *refs),
        grid=(ff // TILE,),
        in_specs=[SMEM]
        + [pl.BlockSpec(v.shape, lambda n: (0, 0)) for v in lefts]
        + [right] * 4
        + [part] * len(sent),
        out_specs=pl.BlockSpec((16, 2, 16, TILE), lambda n: (0, 0, 0, n)),
        out_shape=jax.ShapeDtypeStruct((16, 2, 16, ff), F32),
        scratch_shapes=[
            pltpu.VMEM((1024, 2 * tokens), BF16),
            pltpu.VMEM((1024, 256), BF16),
            pltpu.VMEM((512, 2 * tokens), BF16),
        ],
        cost_estimate=cost(3 * 2 * 768 * 2 * tokens * ff, *rights, *lefts, rights[0], weight=weight),
        compiler_params=params(),
    )(party, *lefts, *rights, *sent)


def store_split(value, stack):
    rows = value.shape[0]
    for xl in range(2):
        cols = [value[:, (2 * y + xl) * 128 :][:, :128] for y in range(4)]
        at = slice(xl * 512, xl * 512 + 512)
        stack[:rows, at], stack[rows:, at] = halves(jnp.concatenate(cols, axis=1))


def add_product(c_ref, w0_ref, w1_ref, out, stack):
    w = jnp.concatenate([w0_ref[...], w1_ref[...]], axis=0)
    out[...] = c_ref[...] + passes(stack, w)


def local_kernel(a_ref, w0_ref, w1_ref, c_ref, out, stack):
    @pl.when(pl.program_id(0) == 0)
    def _():
        store_split(a_ref[...], stack)

    add_product(c_ref, w0_ref, w1_ref, out, stack)


def opened_kernel(x_ref, a_ref, got_ref, w0_ref, w1_ref, c_ref, out, stack):
    @pl.when(pl.program_id(0) == 0)
    def _():
        store_split((x_ref[...] - a_ref[...]) + got_ref[...], stack)

    add_product(c_ref, w0_ref, w1_ref, out, stack)


def forward_call(kernel, lefts, weights, at, c):
    rows, ff = c.shape
    d = lefts[0].shape[1]
    steps = ff // TILE
    tile = pl.BlockSpec((rows, TILE), lambda n: (0, n))
    return pl.pallas_call(
        kernel,
        grid=(steps,),
        in_specs=[pl.BlockSpec((rows, d), lambda n: (0, 0))] * len(lefts)
        + [
            pl.BlockSpec((d // 2, TILE), lambda n: (0, at * steps + n)),
            pl.BlockSpec((d // 2, TILE), lambda n: (0, (at + 2) * steps + n)),
            tile,
        ],
        out_specs=tile,
        out_shape=jax.ShapeDtypeStruct(c.shape, F32),
        scratch_shapes=[pltpu.VMEM((2 * rows, d), BF16)],
        cost_estimate=cost(3 * 2 * rows * d * ff, weights, c, weight=LATE),
        compiler_params=params(),
    )(*lefts, weights, weights, c)


def scattered_pair(a, a_axis, a_dim, b, b_axis, b_dim, first=(), last=()):
    sums, got = [], [[], []]
    for v, axis, dim in ((a, a_axis, a_dim), (b, b_axis, b_dim)):
        here = lax.axis_index(axis)
        sums.append(lax.dynamic_index_in_dim(v, here, dim, keepdims=False))
    for step in (2, 1, 3):
        for n, (v, axis, dim) in enumerate(((a, a_axis, a_dim), (b, b_axis, b_dim))):
            here = lax.axis_index(axis)
            piece = lax.dynamic_index_in_dim(v, (here + step) % 4, dim, keepdims=False)
            if len(got[n]) < 2:
                piece = after(piece, *first)
            else:
                piece = after(piece, got[n][0], *last)
            got[n].append(lax.ppermute(piece, axis, [(i, (i + step) % 4) for i in range(4)]))
    return [s + r[0] + r[1] + r[2] for s, r in zip(sums, got)]


def body(x_share, w_share, g_share, fwd_a, fwd_b, fwd_c, bwd_a, bwd_b, bwd_c):
    x, w, g = x_share[0], w_share[0], g_share[0]
    fa, fb, fc = fwd_a[0], fwd_b[0], fwd_c[0]
    ba, bb, bc = bwd_a[0], bwd_b[0], bwd_c[0]
    party = lax.axis_index("party")
    party0 = party == 0
    first = party0.astype(F32)
    party_id = party.astype(jnp.int32).reshape(1)
    core_id = lax.axis_index("core").astype(jnp.int32).reshape(1)
    xl0 = lax.axis_index("xl") == 0
    ff = w.shape[1]

    x_mine0, x_mine1, x_theirs = turned(core_id, x)
    x0 = lax.ppermute(x_mine0, "party", SWAP)
    x_other = lax.ppermute(x_theirs, "core", SWAP)
    xs0 = jnp.concatenate([x_mine0, x_other[0]], axis=1)
    xs1 = jnp.concatenate([x_mine1, x_other[1]], axis=1)
    a_mine0, a_mine1, a_theirs = turned(core_id, after(ba, x_other))
    a_other = lax.ppermute(a_theirs, "core", SWAP)
    aa0 = jnp.concatenate([a_mine0, a_other[0]], axis=1)
    aa1 = jnp.concatenate([a_mine1, a_other[1]], axis=1)
    d = w - fb
    d_party = lax.ppermute(d, "party", SWAP)
    near = lax.ppermute(jnp.concatenate([fb, d], axis=1), "xl", SWAP)
    d_across = lax.ppermute(d, ("party", "xl"), [(0, 3), (3, 0), (1, 2), (2, 1)])
    d_party, near, d_across = lax.optimization_barrier((d_party, near, d_across, x_theirs))[:3]
    delta = d + d_party
    delta_near = near[:, ff:] + d_across
    packed = jnp.concatenate([fb + first * delta, delta], axis=1)
    packed_near = jnp.concatenate([near[:, :ff] + first * delta_near, delta_near], axis=1)
    weights = jnp.concatenate(
        [jnp.where(xl0, packed, packed_near), jnp.where(xl0, packed_near, packed)], axis=1
    )
    weights = lax.all_gather(after(weights, x0, x_other, a_other), ("y", "z", "core"), axis=0, tiled=True)

    last = g[3 * g.shape[0] // 4 :]
    last = jnp.concatenate([last[:, : ff // 2], last[:, ff // 2 :]], axis=0)
    sent0 = jnp.concatenate([x_other[0], jnp.where(party0, last, aa0)], axis=1)
    got0 = lax.ppermute(sent0, "party", SWAP)
    sent1 = jnp.concatenate(
        [
            xs1[:, :384],
            jnp.where(party0, xs1[:, 384:512], aa1[:, :128]),
            xs1[:, 512:896],
            jnp.where(party0, xs1[:, 896:], aa1[:, 512:640]),
            aa1[:, 128:384],
            aa1[:, 640:896],
        ],
        axis=1,
    )
    got1 = lax.ppermute(sent1, "party", SWAP)
    u = x - fa
    u = lax.ppermute(after(u, got0), "party", SWAP)

    g_other = lax.ppermute(after(g, a_theirs), "core", SWAP)
    b_other = lax.ppermute(after(bb, a_theirs), "core", SWAP)
    rights = (g, bb, g_other, b_other)
    early = grad_parts(party_id, xs0, aa0, (x0, got0), rights, (), 1)
    sent = (got0, lax.ppermute(after(got0, early), "core", SWAP))
    late = grad_parts(party_id, xs1, aa1, (got1,), rights, sent, LATE)

    early = lax.psum_scatter(early.reshape(4, 4, 32, ff), "z", scatter_dimension=0, tiled=True)
    early = lax.psum_scatter(early[0], "y", scatter_dimension=0, tiled=True)
    early = early.reshape(2, 2, 8, ff)
    outputs = forward_call(local_kernel, (fa,), weights, 1, fc)
    late = late.reshape(4, 4, 2, 16, ff)
    part0, part1 = scattered_pair(late[:, :, 0], "z", 0, late[:, :, 1], "y", 1, (), (outputs,))
    part0, part1 = scattered_pair(part0, "y", 0, part1, "z", 0, (u,))
    late = jnp.stack([part0, part1]).reshape(2, 2, 8, ff)
    both = jnp.concatenate([early, late], axis=2)
    spot = 2 * party + lax.axis_index("xl")

    def piece(at):
        return lax.dynamic_index_in_dim(both.reshape(4, *bc.shape), at % 4, 0, keepdims=False)

    grad = piece(spot) + first * bc
    for step in (2, 1, 3):
        give = piece(spot + step)
        if step == 2:
            give = give - first * bc
        grad = grad + lax.ppermute(
            give, ("party", "xl"), [(i, (i + step) % 4) for i in range(4)]
        )

    outputs = forward_call(opened_kernel, (x, fa, u), weights, 0, outputs)
    return (outputs[None], grad[None])


def solution(mesh):
    split = Mesh(
        mesh.devices.reshape(mesh.shape["party"], 4, 2, 4, 2),
        ("party", *DP),
    )
    spec = P("party", DP, None)
    return jax.shard_map(
        body, mesh=split, in_specs=(spec,) * 9, out_specs=(spec, spec), check_vma=False
    )
```

```python
import jax
import jax.numpy as jnp
from jax import lax
from jax.experimental import pallas as pl
from jax.experimental.pallas import tpu as pltpu
from jax.sharding import Mesh
from jax.sharding import PartitionSpec as P

DP = ("y", "xl", "z", "core")
SWAP = [(0, 1), (1, 0)]
F32 = jnp.float32
BF16 = jnp.bfloat16
SMEM = pl.BlockSpec(memory_space=pltpu.SMEM)
TILE = 512
LATE, BESIDE = 8, 1


def cost(flops, *arrays, weight=1):
    moved = sum(4 * a.size for a in arrays)
    return pl.CostEstimate(
        flops=weight * flops, bytes_accessed=weight * moved, transcendentals=0
    )


def params():
    return pltpu.CompilerParams(vmem_limit_bytes=56 * 1024 * 1024)


def after(value, *earlier):
    return lax.optimization_barrier((value, *earlier))[0]


def halves(a):
    high = a.astype(BF16)
    return high, (a - high.astype(F32)).astype(BF16)


def dot(left, right):
    return jnp.dot(left, right, preferred_element_type=F32)


def turn_kernel(core_ref, src, mine0, mine1, theirs):
    even = core_ref[0] == 0
    t = src[...].T
    for y in range(mine0.shape[1]):
        for xl in range(2):
            for z in range(4):
                for k, mine in enumerate((mine0, mine1)):
                    at = (2 * y + xl) * 128 + z * 32 + k * 8
                    e, o = t[at : at + 8], t[at + 16 : at + 24]
                    mine[z, y, xl] = jnp.where(even, e, o)
                    theirs[k, z, y, xl] = jnp.where(even, o, e)


def turned(core, share):
    tokens = share.shape[0]
    mine = jax.ShapeDtypeStruct((4, 4, 2, 8, tokens), F32)
    mine_spec = pl.BlockSpec((4, 2, 2, 8, tokens), lambda i: (0, i, 0, 0, 0))
    theirs_spec = pl.BlockSpec((2, 4, 2, 2, 8, tokens), lambda i: (0, 0, i, 0, 0, 0))
    mine0, mine1, theirs = pl.pallas_call(
        turn_kernel,
        grid=(2,),
        in_specs=[SMEM, pl.BlockSpec((tokens, 512), lambda i: (0, i))],
        out_specs=[mine_spec, mine_spec, theirs_spec],
        out_shape=[mine, mine, jax.ShapeDtypeStruct((2, *mine.shape), F32)],
        cost_estimate=cost(0, share, share),
        compiler_params=params(),
    )(core, share)
    rows = 128 * 2
    return mine0.reshape(rows, tokens), mine1.reshape(rows, tokens), theirs.reshape(2, rows, tokens)


def passes(stack, right):
    rows = stack.shape[0] // 2
    high, low = halves(right)
    both = dot(stack[...], high)
    return both[:rows] + both[rows:] + dot(stack[:rows], low)


def grad_kernel(split, p_ref, x_ref, a_ref, *refs):
    out, pair, pair_sent, single = refs[-4:]
    got_refs, refs = (refs[:1], refs[1:]) if split else (refs[:3], refs[3:])
    g_ref, b_ref, go_ref, bo_ref = refs[:4]
    sent_refs = refs[4:-4]
    is_first = p_ref[0] == 0

    @pl.when(pl.program_id(0) == 0)
    def _():
        x, a = x_ref[...], a_ref[...]
        if split:
            got, late = got_refs[0][:, :1024], got_refs[0][:, 1024:]
            col = lax.broadcasted_iota(jnp.int32, x.shape, 1)
            kept = jnp.logical_or(jnp.logical_not(is_first), col % 512 < 384)
            zero = jnp.zeros((256, 128), F32)
            second = [got[:, 384:512], late[:, :256], zero, got[:, 896:], late[:, 256:], zero]
            second = jnp.where(is_first, jnp.concatenate(second, axis=1), a)
            got = jnp.where(kept, got, 0.0)
            a_sent = jnp.concatenate([a[:, 384:512], a[:, 896:]], axis=1)
            x_sent = jnp.concatenate([x[:, 384:512], x[:, 896:]], axis=1)
            pair_sent[:256], pair_sent[512:768] = halves(x_sent - a_sent)
            pair_sent[256:512], pair_sent[768:] = halves(a_sent)
        else:
            got = jnp.concatenate([got_refs[0][...], got_refs[1][...]], axis=1)
            second = jnp.where(is_first, got_refs[2][...], a)
        opened = x + got
        pair[:256], pair[512:768] = halves(opened - second)
        pair[256:512], pair[768:] = halves(second)
        single[:256], single[256:] = halves(jnp.where(is_first, a, opened))

    b, bo = b_ref[...], bo_ref[...]
    r = g_ref[...] - jnp.where(is_first, 0.0, b)
    ro = go_ref[...] - jnp.where(is_first, 0.0, bo)
    both = passes(pair, jnp.concatenate([r, ro], axis=0))
    if split:
        sent = jnp.concatenate([ref[...] for ref in sent_refs], axis=0)
        both += passes(pair_sent, jnp.where(is_first, 0.0, sent))
    shared = passes(single, jnp.concatenate([b, bo], axis=0))
    part0 = both[:256] - jnp.where(is_first, shared, 0.0)
    part1 = both[256:] + shared
    out[:, 0] = part0.reshape(16, 16, part0.shape[1])
    out[:, 1] = part1.reshape(16, 16, part1.shape[1])


def grad_parts(party, x, a, got, rights, sent, weight):
    tokens, ff = rights[0].shape
    lefts = (x, a, *got)
    right = pl.BlockSpec((tokens, TILE), lambda n: (0, n))
    per = 1024 // TILE
    part = pl.BlockSpec((128, TILE), lambda n: (n // per, n % per))
    return pl.pallas_call(
        lambda *refs: grad_kernel(bool(sent), *refs),
        grid=(ff // TILE,),
        in_specs=[SMEM]
        + [pl.BlockSpec(v.shape, lambda n: (0, 0)) for v in lefts]
        + [right] * 4
        + [part] * len(sent),
        out_specs=pl.BlockSpec((16, 2, 16, TILE), lambda n: (0, 0, 0, n)),
        out_shape=jax.ShapeDtypeStruct((16, 2, 16, ff), F32),
        scratch_shapes=[
            pltpu.VMEM((1024, 2 * tokens), BF16),
            pltpu.VMEM((1024, 256), BF16),
            pltpu.VMEM((512, 2 * tokens), BF16),
        ],
        cost_estimate=cost(3 * 2 * 768 * 2 * tokens * ff, *rights, *lefts, rights[0], weight=weight),
        compiler_params=params(),
    )(party, *lefts, *rights, *sent)


def store_split(value, stack):
    rows = value.shape[0]
    for xl in range(2):
        cols = [value[:, (2 * y + xl) * 128 :][:, :128] for y in range(4)]
        at = slice(xl * 512, xl * 512 + 512)
        stack[:rows, at], stack[rows:, at] = halves(jnp.concatenate(cols, axis=1))


def add_product(c_ref, w0_ref, w1_ref, out, stack):
    w = jnp.concatenate([w0_ref[...], w1_ref[...]], axis=0)
    out[...] = c_ref[...] + passes(stack, w)


def local_kernel(a_ref, w0_ref, w1_ref, c_ref, out, stack):
    @pl.when(pl.program_id(0) == 0)
    def _():
        store_split(a_ref[...], stack)

    add_product(c_ref, w0_ref, w1_ref, out, stack)


def opened_kernel(x_ref, a_ref, got_ref, w0_ref, w1_ref, c_ref, out, stack):
    @pl.when(pl.program_id(0) == 0)
    def _():
        store_split((x_ref[...] - a_ref[...]) + got_ref[...], stack)

    add_product(c_ref, w0_ref, w1_ref, out, stack)


def forward_call(kernel, lefts, weights, at, c):
    rows, ff = c.shape
    d = lefts[0].shape[1]
    steps = ff // TILE
    tile = pl.BlockSpec((rows, TILE), lambda n: (0, n))
    return pl.pallas_call(
        kernel,
        grid=(steps,),
        in_specs=[pl.BlockSpec((rows, d), lambda n: (0, 0))] * len(lefts)
        + [
            pl.BlockSpec((d // 2, TILE), lambda n: (0, at * steps + n)),
            pl.BlockSpec((d // 2, TILE), lambda n: (0, (at + 2) * steps + n)),
            tile,
        ],
        out_specs=tile,
        out_shape=jax.ShapeDtypeStruct(c.shape, F32),
        scratch_shapes=[pltpu.VMEM((2 * rows, d), BF16)],
        cost_estimate=cost(3 * 2 * rows * d * ff, weights, c, weight=BESIDE),
        compiler_params=params(),
    )(*lefts, weights, weights, c)


def scattered_pair(a, a_axis, a_dim, b, b_axis, b_dim, beside):
    sums, got = [], [[], []]
    for v, axis, dim in ((a, a_axis, a_dim), (b, b_axis, b_dim)):
        here = lax.axis_index(axis)
        own = lax.dynamic_index_in_dim(v, here, dim, keepdims=False)
        sums.append(after(own, *beside))
    for step in (2, 1, 3):
        for n, (v, axis, dim) in enumerate(((a, a_axis, a_dim), (b, b_axis, b_dim))):
            here = lax.axis_index(axis)
            piece = lax.dynamic_index_in_dim(v, (here + step) % 4, dim, keepdims=False)
            if len(got[n]) == 2:
                piece = after(piece, got[n][0])
            got[n].append(lax.ppermute(piece, axis, [(i, (i + step) % 4) for i in range(4)]))
    return [s + r[0] + r[1] + r[2] for s, r in zip(sums, got)]


def body(x_share, w_share, g_share, fwd_a, fwd_b, fwd_c, bwd_a, bwd_b, bwd_c):
    x, w, g = x_share[0], w_share[0], g_share[0]
    fa, fb, fc = fwd_a[0], fwd_b[0], fwd_c[0]
    ba, bb, bc = bwd_a[0], bwd_b[0], bwd_c[0]
    party = lax.axis_index("party")
    party0 = party == 0
    first = party0.astype(F32)
    party_id = party.astype(jnp.int32).reshape(1)
    core_id = lax.axis_index("core").astype(jnp.int32).reshape(1)
    xl0 = lax.axis_index("xl") == 0
    ff = w.shape[1]

    x_mine0, x_mine1, x_theirs = turned(core_id, x)
    x0 = lax.ppermute(x_mine0, "party", SWAP)
    x_other = lax.ppermute(x_theirs, "core", SWAP)
    xs0 = jnp.concatenate([x_mine0, x_other[0]], axis=1)
    xs1 = jnp.concatenate([x_mine1, x_other[1]], axis=1)
    x0_other = lax.ppermute(x_other[0], "party", SWAP)
    a_mine0, a_mine1, a_theirs = turned(core_id, after(ba, x_other))
    a_other = lax.ppermute(a_theirs, "core", SWAP)
    aa0 = jnp.concatenate([a_mine0, a_other[0]], axis=1)
    aa1 = jnp.concatenate([a_mine1, a_other[1]], axis=1)
    d = w - fb
    d_party = lax.ppermute(d, "party", SWAP)
    near = lax.ppermute(jnp.concatenate([fb, d], axis=1), "xl", SWAP)
    d_across = lax.ppermute(d, ("party", "xl"), [(0, 3), (3, 0), (1, 2), (2, 1)])
    d_party, near, d_across = lax.optimization_barrier((d_party, near, d_across, x_theirs))[:3]
    delta = d + d_party
    delta_near = near[:, ff:] + d_across
    packed = jnp.concatenate([fb + first * delta, delta], axis=1)
    packed_near = jnp.concatenate([near[:, :ff] + first * delta_near, delta_near], axis=1)
    weights = jnp.concatenate(
        [jnp.where(xl0, packed, packed_near), jnp.where(xl0, packed_near, packed)], axis=1
    )
    weights = lax.all_gather(after(weights, x0, x0_other), ("y", "z", "core"), axis=0, tiled=True)

    last = g[3 * g.shape[0] // 4 :]
    last = jnp.concatenate([last[:, : ff // 2], last[:, ff // 2 :]], axis=0)
    got0 = lax.ppermute(jnp.where(party0, last, aa0), "party", SWAP)
    sent1 = jnp.concatenate(
        [
            xs1[:, :384],
            jnp.where(party0, xs1[:, 384:512], aa1[:, :128]),
            xs1[:, 512:896],
            jnp.where(party0, xs1[:, 896:], aa1[:, 512:640]),
            aa1[:, 128:384],
            aa1[:, 640:896],
        ],
        axis=1,
    )
    got1 = lax.ppermute(sent1, "party", SWAP)
    u_local = x - fa
    u = lax.ppermute(after(u_local, got0), "party", SWAP)

    g_other = lax.ppermute(after(g, a_theirs), "core", SWAP)
    b_other = lax.ppermute(after(bb, a_theirs), "core", SWAP)
    rights = (g, bb, g_other, b_other)
    early = grad_parts(party_id, after(xs0, u_local), aa0, (x0, x0_other, got0), rights, (), 1)
    sent = (got0, lax.ppermute(after(got0, early), "core", SWAP))
    late = grad_parts(party_id, xs1, aa1, (got1,), rights, sent, LATE)

    early = lax.psum_scatter(early.reshape(16, 32, ff), ("z", "y"), scatter_dimension=0, tiled=True)
    early = early.reshape(2, 2, 8, ff)
    outputs = forward_call(local_kernel, (fa,), weights, 1, fc)
    late = late.reshape(4, 4, 2, 16, ff)
    part0, part1 = scattered_pair(late[:, :, 0], "z", 0, late[:, :, 1], "y", 1, (outputs, u))
    outputs = forward_call(opened_kernel, (x, fa, u), weights, 0, after(outputs, part0, part1))
    part0, part1 = scattered_pair(part0, "y", 0, part1, "z", 0, (outputs,))
    late = jnp.stack([part0, part1]).reshape(2, 2, 8, ff)
    both = jnp.concatenate([early, late], axis=2)
    spot = 2 * party + lax.axis_index("xl")

    def piece(at):
        return lax.dynamic_index_in_dim(both.reshape(4, *bc.shape), at % 4, 0, keepdims=False)

    grad = piece(spot) + first * bc
    for step in (2, 1, 3):
        give = piece(spot + step)
        if step == 2:
            give = give - first * bc
        grad = grad + lax.ppermute(
            give, ("party", "xl"), [(i, (i + step) % 4) for i in range(4)]
        )

    return (outputs[None], grad[None])


def solution(mesh):
    split = Mesh(
        mesh.devices.reshape(mesh.shape["party"], 4, 2, 4, 2),
        ("party", *DP),
    )
    spec = P("party", DP, None)
    return jax.shard_map(
        body, mesh=split, in_specs=(spec,) * 9, out_specs=(spec, spec), check_vma=False
    )
```

```python
import jax
import jax.numpy as jnp
from jax import lax
from jax.experimental import pallas as pl
from jax.experimental.pallas import tpu as pltpu
from jax.sharding import Mesh
from jax.sharding import PartitionSpec as P

DP = ("y", "xl", "z", "core")
SWAP = [(0, 1), (1, 0)]
F32 = jnp.float32
BF16 = jnp.bfloat16
SMEM = pl.BlockSpec(memory_space=pltpu.SMEM)
TILE = 512
LATE, BESIDE = 8, 1


def cost(flops, *arrays, weight=1):
    moved = sum(4 * a.size for a in arrays)
    return pl.CostEstimate(
        flops=weight * flops, bytes_accessed=weight * moved, transcendentals=0
    )


def params():
    return pltpu.CompilerParams(vmem_limit_bytes=56 * 1024 * 1024)


def after(value, *earlier):
    return lax.optimization_barrier((value, *earlier))[0]


def halves(a):
    high = a.astype(BF16)
    return high, (a - high.astype(F32)).astype(BF16)


def dot(left, right):
    return jnp.dot(left, right, preferred_element_type=F32)


def turn_kernel(core_ref, src, mine0, mine1, theirs):
    even = core_ref[0] == 0
    t = src[...].T
    for y in range(mine0.shape[1]):
        for xl in range(2):
            for z in range(4):
                for k, mine in enumerate((mine0, mine1)):
                    at = (2 * y + xl) * 128 + z * 32 + k * 8
                    e, o = t[at : at + 8], t[at + 16 : at + 24]
                    mine[z, y, xl] = jnp.where(even, e, o)
                    theirs[k, z, y, xl] = jnp.where(even, o, e)


def turned(core, share):
    tokens = share.shape[0]
    mine = jax.ShapeDtypeStruct((4, 4, 2, 8, tokens), F32)
    mine_spec = pl.BlockSpec((4, 2, 2, 8, tokens), lambda i: (0, i, 0, 0, 0))
    theirs_spec = pl.BlockSpec((2, 4, 2, 2, 8, tokens), lambda i: (0, 0, i, 0, 0, 0))
    mine0, mine1, theirs = pl.pallas_call(
        turn_kernel,
        grid=(2,),
        in_specs=[SMEM, pl.BlockSpec((tokens, 512), lambda i: (0, i))],
        out_specs=[mine_spec, mine_spec, theirs_spec],
        out_shape=[mine, mine, jax.ShapeDtypeStruct((2, *mine.shape), F32)],
        cost_estimate=cost(0, share, share),
        compiler_params=params(),
    )(core, share)
    rows = 128 * 2
    return mine0.reshape(rows, tokens), mine1.reshape(rows, tokens), theirs.reshape(2, rows, tokens)


def passes(stack, right):
    rows = stack.shape[0] // 2
    high, low = halves(right)
    both = dot(stack[...], high)
    return both[:rows] + both[rows:] + dot(stack[:rows], low)


def grad_kernel(split, p_ref, x_ref, a_ref, *refs):
    pair, pair_sent, single = refs[-3:]
    outs, refs = (refs[-5:-3], refs[:-5]) if split else (refs[-4:-3], refs[:-4])
    got_refs, refs = (refs[:1], refs[1:]) if split else (refs[:2], refs[2:])
    g_ref, b_ref, go_ref, bo_ref = refs[:4]
    sent_refs = refs[4:]
    is_first = p_ref[0] == 0

    @pl.when(pl.program_id(0) == 0)
    def _():
        x, a = x_ref[...], a_ref[...]
        if split:
            got, late = got_refs[0][:, :1024], got_refs[0][:, 1024:]
            col = lax.broadcasted_iota(jnp.int32, x.shape, 1)
            kept = jnp.logical_or(jnp.logical_not(is_first), col % 512 < 384)
            zero = jnp.zeros((256, 128), F32)
            second = [got[:, 384:512], late[:, :256], zero, got[:, 896:], late[:, 256:], zero]
            second = jnp.where(is_first, jnp.concatenate(second, axis=1), a)
            got = jnp.where(kept, got, 0.0)
            a_sent = jnp.concatenate([a[:, 384:512], a[:, 896:]], axis=1)
            x_sent = jnp.concatenate([x[:, 384:512], x[:, 896:]], axis=1)
            pair_sent[:256], pair_sent[512:768] = halves(x_sent - a_sent)
            pair_sent[256:512], pair_sent[768:] = halves(a_sent)
        else:
            got = got_refs[0][...]
            second = jnp.where(is_first, got_refs[1][...], a)
        opened = x + got
        pair[:256], pair[512:768] = halves(opened - second)
        pair[256:512], pair[768:] = halves(second)
        single[:256], single[256:] = halves(jnp.where(is_first, a, opened))

    b, bo = b_ref[...], bo_ref[...]
    r = g_ref[...] - jnp.where(is_first, 0.0, b)
    ro = go_ref[...] - jnp.where(is_first, 0.0, bo)
    both = passes(pair, jnp.concatenate([r, ro], axis=0))
    if split:
        sent = jnp.concatenate([ref[...] for ref in sent_refs], axis=0)
        both += passes(pair_sent, jnp.where(is_first, 0.0, sent))
    shared = passes(single, jnp.concatenate([b, bo], axis=0))
    part0 = both[:256] - jnp.where(is_first, shared, 0.0)
    part1 = both[256:] + shared
    for n, part in enumerate((part0, part1)):
        part = part.reshape(16, 16, part.shape[1])
        if split:
            outs[n][...] = part
        else:
            outs[0][:, n] = part


def grad_parts(party, x, a, got, rights, sent, weight):
    tokens, ff = rights[0].shape
    lefts = (x, a, *got)
    right = pl.BlockSpec((tokens, TILE), lambda n: (0, n))
    per = 1024 // TILE
    part = pl.BlockSpec((128, TILE), lambda n: (n // per, n % per))
    return pl.pallas_call(
        lambda *refs: grad_kernel(bool(sent), *refs),
        grid=(ff // TILE,),
        in_specs=[SMEM]
        + [pl.BlockSpec(v.shape, lambda n: (0, 0)) for v in lefts]
        + [right] * 4
        + [part] * len(sent),
        out_specs=[pl.BlockSpec((16, 16, TILE), lambda n: (0, 0, n))] * 2
        if sent
        else pl.BlockSpec((16, 2, 16, TILE), lambda n: (0, 0, 0, n)),
        out_shape=[jax.ShapeDtypeStruct((16, 16, ff), F32)] * 2
        if sent
        else jax.ShapeDtypeStruct((16, 2, 16, ff), F32),
        scratch_shapes=[
            pltpu.VMEM((1024, 2 * tokens), BF16),
            pltpu.VMEM((1024, 256), BF16),
            pltpu.VMEM((512, 2 * tokens), BF16),
        ],
        cost_estimate=cost(3 * 2 * 768 * 2 * tokens * ff, *rights, *lefts, rights[0], weight=weight),
        compiler_params=params(),
    )(party, *lefts, *rights, *sent)


def store_split(value, stack):
    rows = value.shape[0]
    for xl in range(2):
        cols = [value[:, (2 * y + xl) * 128 :][:, :128] for y in range(4)]
        at = slice(xl * 512, xl * 512 + 512)
        stack[:rows, at], stack[rows:, at] = halves(jnp.concatenate(cols, axis=1))


def add_product(c_ref, w0_ref, w1_ref, out, stack):
    w = jnp.concatenate([w0_ref[...], w1_ref[...]], axis=0)
    out[...] = c_ref[...] + passes(stack, w)


def local_kernel(a_ref, w0_ref, w1_ref, c_ref, out, stack):
    @pl.when(pl.program_id(0) == 0)
    def _():
        store_split(a_ref[...], stack)

    add_product(c_ref, w0_ref, w1_ref, out, stack)


def opened_kernel(x_ref, a_ref, got_ref, w0_ref, w1_ref, c_ref, out, stack):
    @pl.when(pl.program_id(0) == 0)
    def _():
        store_split((x_ref[...] - a_ref[...]) + got_ref[...], stack)

    add_product(c_ref, w0_ref, w1_ref, out, stack)


def forward_call(kernel, lefts, weights, at, c):
    rows, ff = c.shape
    d = lefts[0].shape[1]
    steps = ff // TILE
    tile = pl.BlockSpec((rows, TILE), lambda n: (0, n))
    return pl.pallas_call(
        kernel,
        grid=(steps,),
        in_specs=[pl.BlockSpec((rows, d), lambda n: (0, 0))] * len(lefts)
        + [
            pl.BlockSpec((d // 2, TILE), lambda n: (0, at * steps + n)),
            pl.BlockSpec((d // 2, TILE), lambda n: (0, (at + 2) * steps + n)),
            tile,
        ],
        out_specs=tile,
        out_shape=jax.ShapeDtypeStruct(c.shape, F32),
        scratch_shapes=[pltpu.VMEM((2 * rows, d), BF16)],
        cost_estimate=cost(3 * 2 * rows * d * ff, weights, c, weight=BESIDE),
        compiler_params=params(),
    )(*lefts, weights, weights, c)


def scattered_pair(a, a_axis, a_dim, b, b_axis, b_dim, beside):
    sums, got = [], [[], []]
    for v, axis, dim in ((a, a_axis, a_dim), (b, b_axis, b_dim)):
        here = lax.axis_index(axis)
        own = lax.dynamic_index_in_dim(v, here, dim, keepdims=False)
        sums.append(after(own, *beside) if beside else own)
    for step in (2, 1, 3):
        for n, (v, axis, dim) in enumerate(((a, a_axis, a_dim), (b, b_axis, b_dim))):
            here = lax.axis_index(axis)
            piece = lax.dynamic_index_in_dim(v, (here + step) % 4, dim, keepdims=False)
            if len(got[n]) == 2:
                piece = after(piece, got[n][0])
            got[n].append(lax.ppermute(piece, axis, [(i, (i + step) % 4) for i in range(4)]))
    return [s + r[0] + r[1] + r[2] for s, r in zip(sums, got)]


def body(x_share, w_share, g_share, fwd_a, fwd_b, fwd_c, bwd_a, bwd_b, bwd_c):
    x, w, g = x_share[0], w_share[0], g_share[0]
    fa, fb, fc = fwd_a[0], fwd_b[0], fwd_c[0]
    ba, bb, bc = bwd_a[0], bwd_b[0], bwd_c[0]
    party = lax.axis_index("party")
    party0 = party == 0
    first = party0.astype(F32)
    party_id = party.astype(jnp.int32).reshape(1)
    core_id = lax.axis_index("core").astype(jnp.int32).reshape(1)
    xl0 = lax.axis_index("xl") == 0
    ff = w.shape[1]

    x_mine0, x_mine1, x_theirs = turned(core_id, x)
    x_other = lax.ppermute(x_theirs, "core", SWAP)
    xs0 = jnp.concatenate([x_mine0, x_other[0]], axis=1)
    xs1 = jnp.concatenate([x_mine1, x_other[1]], axis=1)
    x0 = lax.ppermute(xs0, "party", SWAP)
    a_mine0, a_mine1, a_theirs = turned(core_id, after(ba, x_theirs))
    a_other = lax.ppermute(a_theirs, "core", SWAP)
    aa0 = jnp.concatenate([a_mine0, a_other[0]], axis=1)
    aa1 = jnp.concatenate([a_mine1, a_other[1]], axis=1)
    last = g[3 * g.shape[0] // 4 :]
    last = jnp.concatenate([last[:, : ff // 2], last[:, ff // 2 :]], axis=0)
    sent0 = jnp.where(party0, last, aa0)
    got0 = lax.ppermute(sent0, "party", SWAP)
    sent1 = jnp.concatenate(
        [
            xs1[:, :384],
            jnp.where(party0, xs1[:, 384:512], aa1[:, :128]),
            xs1[:, 512:896],
            jnp.where(party0, xs1[:, 896:], aa1[:, 512:640]),
            aa1[:, 128:384],
            aa1[:, 640:896],
        ],
        axis=1,
    )
    d = w - fb
    d_party = lax.ppermute(d, "party", SWAP)
    near = lax.ppermute(jnp.concatenate([fb, d], axis=1), "xl", SWAP)
    d_across = lax.ppermute(d, ("party", "xl"), [(0, 3), (3, 0), (1, 2), (2, 1)])
    d_party, near, d_across = lax.optimization_barrier((d_party, near, d_across, sent0, sent1))[:3]
    delta = d + d_party
    delta_near = near[:, ff:] + d_across
    packed = jnp.concatenate([fb + first * delta, delta], axis=1)
    packed_near = jnp.concatenate([near[:, :ff] + first * delta_near, delta_near], axis=1)
    weights = jnp.concatenate(
        [jnp.where(xl0, packed, packed_near), jnp.where(xl0, packed_near, packed)], axis=1
    )
    weights = lax.all_gather(after(weights, x0), ("y", "z", "core"), axis=0, tiled=True)

    got1 = lax.ppermute(sent1, "party", SWAP)
    u_local = x - fa
    u = lax.ppermute(after(u_local, got0), "party", SWAP)

    g_other = lax.ppermute(after(g, a_other), "core", SWAP)
    b_other = lax.ppermute(after(bb, a_other), "core", SWAP)
    rights = (g, bb, g_other, b_other)
    early = grad_parts(party_id, after(xs0, u_local), aa0, (x0, got0), rights, (), 1)
    sent = (got0, lax.ppermute(after(got0, early), "core", SWAP))
    late = grad_parts(party_id, xs1, aa1, (got1,), rights, sent, LATE)

    early = lax.psum_scatter(early.reshape(16, 32, ff), ("z", "y"), scatter_dimension=0, tiled=True)
    early = early.reshape(2, 2, 8, ff)
    outputs = forward_call(local_kernel, (fa,), weights, 1, fc)
    part0, part1 = (part.reshape(4, 4, 16, ff) for part in late)
    part0, part1 = scattered_pair(part0, "z", 0, part1, "y", 1, (outputs, u))
    part0, part1 = scattered_pair(part0, "y", 0, part1, "z", 0, ())
    late = jnp.stack([part0, part1]).reshape(2, 2, 8, ff)
    both = jnp.concatenate([early, late], axis=2)
    outputs = forward_call(opened_kernel, (x, fa, u), weights, 0, after(outputs, both))
    spot = 2 * party + lax.axis_index("xl")

    def piece(at):
        return lax.dynamic_index_in_dim(both.reshape(4, *bc.shape), at % 4, 0, keepdims=False)

    grad = piece(spot) + first * bc
    for step in (2, 1, 3):
        give = piece(spot + step)
        if step == 2:
            give = give - first * bc
        grad = grad + lax.ppermute(
            give, ("party", "xl"), [(i, (i + step) % 4) for i in range(4)]
        )

    return (outputs[None], grad[None])


def solution(mesh):
    split = Mesh(
        mesh.devices.reshape(mesh.shape["party"], 4, 2, 4, 2),
        ("party", *DP),
    )
    spec = P("party", DP, None)
    return jax.shard_map(
        body, mesh=split, in_specs=(spec,) * 9, out_specs=(spec, spec), check_vma=False
    )
```

```python
import jax
import jax.numpy as jnp
from jax import lax
from jax.experimental import pallas as pl
from jax.experimental.pallas import tpu as pltpu
from jax.sharding import Mesh
from jax.sharding import PartitionSpec as P

DP = ("y", "xl", "z", "core")
SWAP = [(0, 1), (1, 0)]
F32 = jnp.float32
BF16 = jnp.bfloat16
SMEM = pl.BlockSpec(memory_space=pltpu.SMEM)
TILE = 512
LATE, BESIDE = 8, 1


def cost(flops, *arrays, weight=1):
    moved = sum(4 * a.size for a in arrays)
    return pl.CostEstimate(
        flops=weight * flops, bytes_accessed=weight * moved, transcendentals=0
    )


def params():
    return pltpu.CompilerParams(vmem_limit_bytes=56 * 1024 * 1024)


def after(value, *earlier):
    return lax.optimization_barrier((value, *earlier))[0]


def halves(a):
    high = a.astype(BF16)
    return high, (a - high.astype(F32)).astype(BF16)


def dot(left, right):
    return jnp.dot(left, right, preferred_element_type=F32)


def turn_kernel(core_ref, src, mine0, mine1, theirs):
    even = core_ref[0] == 0
    t = src[...].T
    for y in range(mine0.shape[1]):
        for xl in range(2):
            for z in range(4):
                for k, mine in enumerate((mine0, mine1)):
                    at = (2 * y + xl) * 128 + z * 32 + k * 8
                    e, o = t[at : at + 8], t[at + 16 : at + 24]
                    mine[z, y, xl] = jnp.where(even, e, o)
                    theirs[k, z, y, xl] = jnp.where(even, o, e)


def turned(core, share):
    tokens = share.shape[0]
    mine = jax.ShapeDtypeStruct((4, 4, 2, 8, tokens), F32)
    mine_spec = pl.BlockSpec((4, 2, 2, 8, tokens), lambda i: (0, i, 0, 0, 0))
    theirs_spec = pl.BlockSpec((2, 4, 2, 2, 8, tokens), lambda i: (0, 0, i, 0, 0, 0))
    mine0, mine1, theirs = pl.pallas_call(
        turn_kernel,
        grid=(2,),
        in_specs=[SMEM, pl.BlockSpec((tokens, 512), lambda i: (0, i))],
        out_specs=[mine_spec, mine_spec, theirs_spec],
        out_shape=[mine, mine, jax.ShapeDtypeStruct((2, *mine.shape), F32)],
        cost_estimate=cost(0, share, share),
        compiler_params=params(),
    )(core, share)
    rows = 128 * 2
    return mine0.reshape(rows, tokens), mine1.reshape(rows, tokens), theirs.reshape(2, rows, tokens)


def passes(stack, right):
    rows = stack.shape[0] // 2
    high, low = halves(right)
    both = dot(stack[...], high)
    return both[:rows] + both[rows:] + dot(stack[:rows], low)


def grad_kernel(split, p_ref, x_ref, a_ref, *refs):
    pair, pair_sent, single = refs[-3:]
    outs, refs = (refs[-5:-3], refs[:-5]) if split else (refs[-4:-3], refs[:-4])
    got_refs, refs = (refs[:1], refs[1:]) if split else (refs[:2], refs[2:])
    g_ref, b_ref, go_ref, bo_ref = refs[:4]
    sent_refs = refs[4:]
    is_first = p_ref[0] == 0

    @pl.when(pl.program_id(0) == 0)
    def _():
        x, a = x_ref[...], a_ref[...]
        if split:
            got, late = got_refs[0][:, :1024], got_refs[0][:, 1024:]
            col = lax.broadcasted_iota(jnp.int32, x.shape, 1)
            kept = jnp.logical_or(jnp.logical_not(is_first), col % 512 < 384)
            zero = jnp.zeros((256, 128), F32)
            second = [got[:, 384:512], late[:, :256], zero, got[:, 896:], late[:, 256:], zero]
            second = jnp.where(is_first, jnp.concatenate(second, axis=1), a)
            got = jnp.where(kept, got, 0.0)
            a_sent = jnp.concatenate([a[:, 384:512], a[:, 896:]], axis=1)
            x_sent = jnp.concatenate([x[:, 384:512], x[:, 896:]], axis=1)
            pair_sent[:256], pair_sent[512:768] = halves(x_sent - a_sent)
            pair_sent[256:512], pair_sent[768:] = halves(a_sent)
        else:
            got = got_refs[0][...]
            second = jnp.where(is_first, got_refs[1][...], a)
        opened = x + got
        pair[:256], pair[512:768] = halves(opened - second)
        pair[256:512], pair[768:] = halves(second)
        single[:256], single[256:] = halves(jnp.where(is_first, a, opened))

    b, bo = b_ref[...], bo_ref[...]
    r = g_ref[...] - jnp.where(is_first, 0.0, b)
    ro = go_ref[...] - jnp.where(is_first, 0.0, bo)
    both = passes(pair, jnp.concatenate([r, ro], axis=0))
    if split:
        sent = jnp.concatenate([ref[...] for ref in sent_refs], axis=0)
        both += passes(pair_sent, jnp.where(is_first, 0.0, sent))
    shared = passes(single, jnp.concatenate([b, bo], axis=0))
    part0 = both[:256] - jnp.where(is_first, shared, 0.0)
    part1 = both[256:] + shared
    for n, part in enumerate((part0, part1)):
        part = part.reshape(16, 16, part.shape[1])
        if split:
            outs[n][...] = part
        else:
            outs[0][:, n] = part


def grad_parts(party, x, a, got, rights, sent, weight):
    tokens, ff = rights[0].shape
    lefts = (x, a, *got)
    right = pl.BlockSpec((tokens, TILE), lambda n: (0, n))
    per = 1024 // TILE
    part = pl.BlockSpec((128, TILE), lambda n: (n // per, n % per))
    return pl.pallas_call(
        lambda *refs: grad_kernel(bool(sent), *refs),
        grid=(ff // TILE,),
        in_specs=[SMEM]
        + [pl.BlockSpec(v.shape, lambda n: (0, 0)) for v in lefts]
        + [right] * 4
        + [part] * len(sent),
        out_specs=[pl.BlockSpec((16, 16, TILE), lambda n: (0, 0, n))] * 2
        if sent
        else pl.BlockSpec((16, 2, 16, TILE), lambda n: (0, 0, 0, n)),
        out_shape=[jax.ShapeDtypeStruct((16, 16, ff), F32)] * 2
        if sent
        else jax.ShapeDtypeStruct((16, 2, 16, ff), F32),
        scratch_shapes=[
            pltpu.VMEM((1024, 2 * tokens), BF16),
            pltpu.VMEM((1024, 256), BF16),
            pltpu.VMEM((512, 2 * tokens), BF16),
        ],
        cost_estimate=cost(3 * 2 * 768 * 2 * tokens * ff, *rights, *lefts, rights[0], weight=weight),
        compiler_params=params(),
    )(party, *lefts, *rights, *sent)


def store_split(value, stack):
    rows = value.shape[0]
    for xl in range(2):
        cols = [value[:, (2 * y + xl) * 128 :][:, :128] for y in range(4)]
        at = slice(xl * 512, xl * 512 + 512)
        stack[:rows, at], stack[rows:, at] = halves(jnp.concatenate(cols, axis=1))


def add_product(c_ref, w0_ref, w1_ref, out, stack):
    w = jnp.concatenate([w0_ref[...], w1_ref[...]], axis=0)
    out[...] = c_ref[...] + passes(stack, w)


def local_kernel(a_ref, w0_ref, w1_ref, c_ref, out, stack):
    @pl.when(pl.program_id(0) == 0)
    def _():
        store_split(a_ref[...], stack)

    add_product(c_ref, w0_ref, w1_ref, out, stack)


def opened_kernel(x_ref, a_ref, got_ref, w0_ref, w1_ref, c_ref, out, stack):
    @pl.when(pl.program_id(0) == 0)
    def _():
        store_split((x_ref[...] - a_ref[...]) + got_ref[...], stack)

    add_product(c_ref, w0_ref, w1_ref, out, stack)


def forward_call(kernel, lefts, weights, at, c):
    rows, ff = c.shape
    d = lefts[0].shape[1]
    steps = ff // TILE
    tile = pl.BlockSpec((rows, TILE), lambda n: (0, n))
    return pl.pallas_call(
        kernel,
        grid=(steps,),
        in_specs=[pl.BlockSpec((rows, d), lambda n: (0, 0))] * len(lefts)
        + [
            pl.BlockSpec((d // 2, TILE), lambda n: (0, at * steps + n)),
            pl.BlockSpec((d // 2, TILE), lambda n: (0, (at + 2) * steps + n)),
            tile,
        ],
        out_specs=tile,
        out_shape=jax.ShapeDtypeStruct(c.shape, F32),
        scratch_shapes=[pltpu.VMEM((2 * rows, d), BF16)],
        cost_estimate=cost(3 * 2 * rows * d * ff, weights, c, weight=BESIDE),
        compiler_params=params(),
    )(*lefts, weights, weights, c)


def scattered_pair(a, a_axis, a_dim, b, b_axis, b_dim, between=(), beside=None):
    sums, got = [], [[], []]
    for v, axis, dim in ((a, a_axis, a_dim), (b, b_axis, b_dim)):
        here = lax.axis_index(axis)
        sums.append(lax.dynamic_index_in_dim(v, here, dim, keepdims=False))
    for step in (2, 1, 3):
        for n, (v, axis, dim) in enumerate(((a, a_axis, a_dim), (b, b_axis, b_dim))):
            here = lax.axis_index(axis)
            piece = lax.dynamic_index_in_dim(v, (here + step) % 4, dim, keepdims=False)
            if len(got[n]) == 2:
                piece = after(piece, got[n][0], *between)
            got[n].append(lax.ppermute(piece, axis, [(i, (i + step) % 4) for i in range(4)]))
    made = None
    if beside:
        made = beside(got[0][0], got[1][0])
        sums = [after(s, made) for s in sums]
    return [s + r[0] + r[1] + r[2] for s, r in zip(sums, got)], made


def body(x_share, w_share, g_share, fwd_a, fwd_b, fwd_c, bwd_a, bwd_b, bwd_c):
    x, w, g = x_share[0], w_share[0], g_share[0]
    fa, fb, fc = fwd_a[0], fwd_b[0], fwd_c[0]
    ba, bb, bc = bwd_a[0], bwd_b[0], bwd_c[0]
    party = lax.axis_index("party")
    party0 = party == 0
    first = party0.astype(F32)
    party_id = party.astype(jnp.int32).reshape(1)
    core_id = lax.axis_index("core").astype(jnp.int32).reshape(1)
    xl0 = lax.axis_index("xl") == 0
    ff = w.shape[1]

    x_mine0, x_mine1, x_theirs = turned(core_id, x)
    x_other = lax.ppermute(x_theirs, "core", SWAP)
    xs0 = jnp.concatenate([x_mine0, x_other[0]], axis=1)
    xs1 = jnp.concatenate([x_mine1, x_other[1]], axis=1)
    x0 = lax.ppermute(xs0, "party", SWAP)
    a_mine0, a_mine1, a_theirs = turned(core_id, after(ba, x_theirs))
    a_other = lax.ppermute(a_theirs, "core", SWAP)
    aa0 = jnp.concatenate([a_mine0, a_other[0]], axis=1)
    aa1 = jnp.concatenate([a_mine1, a_other[1]], axis=1)
    last = g[3 * g.shape[0] // 4 :]
    last = jnp.concatenate([last[:, : ff // 2], last[:, ff // 2 :]], axis=0)
    sent0 = jnp.where(party0, last, aa0)
    got0 = lax.ppermute(sent0, "party", SWAP)
    sent1 = jnp.concatenate(
        [
            xs1[:, :384],
            jnp.where(party0, xs1[:, 384:512], aa1[:, :128]),
            xs1[:, 512:896],
            jnp.where(party0, xs1[:, 896:], aa1[:, 512:640]),
            aa1[:, 128:384],
            aa1[:, 640:896],
        ],
        axis=1,
    )
    d = w - fb
    d_party = lax.ppermute(d, "party", SWAP)
    near = lax.ppermute(jnp.concatenate([fb, d], axis=1), "xl", SWAP)
    d_across = lax.ppermute(d, ("party", "xl"), [(0, 3), (3, 0), (1, 2), (2, 1)])
    d_party, near, d_across = lax.optimization_barrier((d_party, near, d_across, sent0, sent1))[:3]
    delta = d + d_party
    delta_near = near[:, ff:] + d_across
    packed = jnp.concatenate([fb + first * delta, delta], axis=1)
    packed_near = jnp.concatenate([near[:, :ff] + first * delta_near, delta_near], axis=1)
    weights = jnp.concatenate(
        [jnp.where(xl0, packed, packed_near), jnp.where(xl0, packed_near, packed)], axis=1
    )
    weights = lax.all_gather(after(weights, x0), ("y", "z", "core"), axis=0, tiled=True)

    got1 = lax.ppermute(sent1, "party", SWAP)
    u_local = x - fa
    u = lax.ppermute(after(u_local, got0), "party", SWAP)

    g_other = lax.ppermute(after(g, a_other), "core", SWAP)
    b_other = lax.ppermute(after(bb, a_other), "core", SWAP)
    rights = (g, bb, g_other, b_other)
    early = grad_parts(party_id, after(xs0, u_local, xs1, aa1), aa0, (x0, got0), rights, (), 1)
    sent = (got0, lax.ppermute(after(got0, early), "core", SWAP))
    late = grad_parts(party_id, xs1, aa1, (got1,), rights, sent, LATE)

    early = lax.psum_scatter(early.reshape(16, 32, ff), ("z", "y"), scatter_dimension=0, tiled=True)
    early = early.reshape(2, 2, 8, ff)
    outputs = forward_call(local_kernel, (fa,), weights, 1, fc)
    part0, part1 = (part.reshape(4, 4, 16, ff) for part in late)

    def opened(*earlier):
        return forward_call(opened_kernel, (x, fa, u), weights, 0, after(outputs, *earlier))

    (part0, part1), y = scattered_pair(part0, "z", 0, part1, "y", 1, (outputs,), opened)
    (part0, part1), _ = scattered_pair(part0, "y", 0, part1, "z", 0)
    late = jnp.stack([part0, part1]).reshape(2, 2, 8, ff)
    both = jnp.concatenate([early, late], axis=2)
    spot = 2 * party + lax.axis_index("xl")

    def piece(at):
        return lax.dynamic_index_in_dim(both.reshape(4, *bc.shape), at % 4, 0, keepdims=False)

    grad = piece(spot) + first * bc
    for step in (2, 1, 3):
        give = piece(spot + step)
        if step == 2:
            give = give - first * bc
        grad = grad + lax.ppermute(
            give, ("party", "xl"), [(i, (i + step) % 4) for i in range(4)]
        )

    return (y[None], grad[None])


def solution(mesh):
    split = Mesh(
        mesh.devices.reshape(mesh.shape["party"], 4, 2, 4, 2),
        ("party", *DP),
    )
    spec = P("party", DP, None)
    return jax.shard_map(
        body, mesh=split, in_specs=(spec,) * 9, out_specs=(spec, spec), check_vma=False
    )
```

```python
import jax
import jax.numpy as jnp
from jax import lax
from jax.experimental import pallas as pl
from jax.experimental.pallas import tpu as pltpu
from jax.sharding import Mesh
from jax.sharding import PartitionSpec as P

DP = ("y", "xl", "z", "core")
SWAP = [(0, 1), (1, 0)]
F32 = jnp.float32
BF16 = jnp.bfloat16
SMEM = pl.BlockSpec(memory_space=pltpu.SMEM)
TILE = 512
LATE, BESIDE = 8, 1


def cost(flops, *arrays, weight=1):
    moved = sum(4 * a.size for a in arrays)
    return pl.CostEstimate(
        flops=weight * flops, bytes_accessed=weight * moved, transcendentals=0
    )


def params():
    return pltpu.CompilerParams(vmem_limit_bytes=56 * 1024 * 1024)


def after(value, *earlier):
    return lax.optimization_barrier((value, *earlier))[0]


def halves(a):
    high = a.astype(BF16)
    return high, (a - high.astype(F32)).astype(BF16)


def dot(left, right):
    return jnp.dot(left, right, preferred_element_type=F32)


def turn_kernel(core_ref, src, mine0, mine1, theirs):
    even = core_ref[0] == 0
    t = src[...].T
    for y in range(mine0.shape[1]):
        for xl in range(2):
            for z in range(4):
                for k, mine in enumerate((mine0, mine1)):
                    at = (2 * y + xl) * 128 + z * 32 + k * 8
                    e, o = t[at : at + 8], t[at + 16 : at + 24]
                    mine[z, y, xl] = jnp.where(even, e, o)
                    theirs[k, z, y, xl] = jnp.where(even, o, e)


def turned(core, share):
    tokens = share.shape[0]
    mine = jax.ShapeDtypeStruct((4, 4, 2, 8, tokens), F32)
    mine_spec = pl.BlockSpec((4, 2, 2, 8, tokens), lambda i: (0, i, 0, 0, 0))
    theirs_spec = pl.BlockSpec((2, 4, 2, 2, 8, tokens), lambda i: (0, 0, i, 0, 0, 0))
    mine0, mine1, theirs = pl.pallas_call(
        turn_kernel,
        grid=(2,),
        in_specs=[SMEM, pl.BlockSpec((tokens, 512), lambda i: (0, i))],
        out_specs=[mine_spec, mine_spec, theirs_spec],
        out_shape=[mine, mine, jax.ShapeDtypeStruct((2, *mine.shape), F32)],
        cost_estimate=cost(0, share, share),
        compiler_params=params(),
    )(core, share)
    rows = 128 * 2
    return mine0.reshape(rows, tokens), mine1.reshape(rows, tokens), theirs.reshape(2, rows, tokens)


def passes(stack, right):
    rows = stack.shape[0] // 2
    high, low = halves(right)
    both = dot(stack[...], high)
    return both[:rows] + both[rows:] + dot(stack[:rows], low)


def grad_kernel(split, p_ref, x_ref, a_ref, *refs):
    pair, pair_sent, single = refs[-3:]
    outs, refs = (refs[-5:-3], refs[:-5]) if split else (refs[-4:-3], refs[:-4])
    got_refs, refs = (refs[:1], refs[1:]) if split else (refs[:2], refs[2:])
    g_ref, b_ref, go_ref, bo_ref = refs[:4]
    sent_refs = refs[4:]
    is_first = p_ref[0] == 0

    @pl.when(pl.program_id(0) == 0)
    def _():
        x, a = x_ref[...], a_ref[...]
        if split:
            got, late = got_refs[0][:, :1024], got_refs[0][:, 1024:]
            col = lax.broadcasted_iota(jnp.int32, x.shape, 1)
            kept = jnp.logical_or(jnp.logical_not(is_first), col % 512 < 384)
            zero = jnp.zeros((256, 128), F32)
            second = [got[:, 384:512], late[:, :256], zero, got[:, 896:], late[:, 256:], zero]
            second = jnp.where(is_first, jnp.concatenate(second, axis=1), a)
            got = jnp.where(kept, got, 0.0)
            a_sent = jnp.concatenate([a[:, 384:512], a[:, 896:]], axis=1)
            x_sent = jnp.concatenate([x[:, 384:512], x[:, 896:]], axis=1)
            pair_sent[:256], pair_sent[512:768] = halves(x_sent - a_sent)
            pair_sent[256:512], pair_sent[768:] = halves(a_sent)
        else:
            got = got_refs[0][...]
            second = jnp.where(is_first, got_refs[1][...], a)
        opened = x + got
        pair[:256], pair[512:768] = halves(opened - second)
        pair[256:512], pair[768:] = halves(second)
        single[:256], single[256:] = halves(jnp.where(is_first, a, opened))

    b, bo = b_ref[...], bo_ref[...]
    r = g_ref[...] - jnp.where(is_first, 0.0, b)
    ro = go_ref[...] - jnp.where(is_first, 0.0, bo)
    both = passes(pair, jnp.concatenate([r, ro], axis=0))
    if split:
        sent = jnp.concatenate([ref[...] for ref in sent_refs], axis=0)
        both += passes(pair_sent, jnp.where(is_first, 0.0, sent))
    shared = passes(single, jnp.concatenate([b, bo], axis=0))
    part0 = both[:256] - jnp.where(is_first, shared, 0.0)
    part1 = both[256:] + shared
    for n, part in enumerate((part0, part1)):
        part = part.reshape(16, 16, part.shape[1])
        if split:
            outs[n][...] = part
        else:
            outs[0][:, n] = part


def grad_parts(party, x, a, got, rights, sent, weight):
    tokens, ff = rights[0].shape
    lefts = (x, a, *got)
    right = pl.BlockSpec((tokens, TILE), lambda n: (0, n))
    per = 1024 // TILE
    part = pl.BlockSpec((128, TILE), lambda n: (n // per, n % per))
    return pl.pallas_call(
        lambda *refs: grad_kernel(bool(sent), *refs),
        grid=(ff // TILE,),
        in_specs=[SMEM]
        + [pl.BlockSpec(v.shape, lambda n: (0, 0)) for v in lefts]
        + [right] * 4
        + [part] * len(sent),
        out_specs=[pl.BlockSpec((16, 16, TILE), lambda n: (0, 0, n))] * 2
        if sent
        else pl.BlockSpec((16, 2, 16, TILE), lambda n: (0, 0, 0, n)),
        out_shape=[jax.ShapeDtypeStruct((16, 16, ff), F32)] * 2
        if sent
        else jax.ShapeDtypeStruct((16, 2, 16, ff), F32),
        scratch_shapes=[
            pltpu.VMEM((1024, 2 * tokens), BF16),
            pltpu.VMEM((1024, 256), BF16),
            pltpu.VMEM((512, 2 * tokens), BF16),
        ],
        cost_estimate=cost(3 * 2 * 768 * 2 * tokens * ff, *rights, *lefts, rights[0], weight=weight),
        compiler_params=params(),
    )(party, *lefts, *rights, *sent)


def store_split(value, stack):
    rows = value.shape[0]
    for xl in range(2):
        cols = [value[:, (2 * y + xl) * 128 :][:, :128] for y in range(4)]
        at = slice(xl * 512, xl * 512 + 512)
        stack[:rows, at], stack[rows:, at] = halves(jnp.concatenate(cols, axis=1))


def add_product(c_ref, w0_ref, w1_ref, out, stack):
    w = jnp.concatenate([w0_ref[...], w1_ref[...]], axis=0)
    out[...] = c_ref[...] + passes(stack, w)


def local_kernel(a_ref, w0_ref, w1_ref, c_ref, out, stack):
    @pl.when(pl.program_id(0) == 0)
    def _():
        store_split(a_ref[...], stack)

    add_product(c_ref, w0_ref, w1_ref, out, stack)


def opened_kernel(x_ref, a_ref, got_ref, w0_ref, w1_ref, c_ref, out, stack):
    @pl.when(pl.program_id(0) == 0)
    def _():
        store_split((x_ref[...] - a_ref[...]) + got_ref[...], stack)

    add_product(c_ref, w0_ref, w1_ref, out, stack)


def forward_call(kernel, lefts, weights, at, c):
    rows, ff = c.shape
    d = lefts[0].shape[1]
    steps = ff // TILE
    tile = pl.BlockSpec((rows, TILE), lambda n: (0, n))
    return pl.pallas_call(
        kernel,
        grid=(steps,),
        in_specs=[pl.BlockSpec((rows, d), lambda n: (0, 0))] * len(lefts)
        + [
            pl.BlockSpec((d // 2, TILE), lambda n: (0, at * steps + n)),
            pl.BlockSpec((d // 2, TILE), lambda n: (0, (at + 2) * steps + n)),
            tile,
        ],
        out_specs=tile,
        out_shape=jax.ShapeDtypeStruct(c.shape, F32),
        scratch_shapes=[pltpu.VMEM((2 * rows, d), BF16)],
        cost_estimate=cost(3 * 2 * rows * d * ff, weights, c, weight=BESIDE),
        compiler_params=params(),
    )(*lefts, weights, weights, c)


def scattered_pair(a, a_axis, a_dim, b, b_axis, b_dim, between=(), beside=None):
    sums, got = [], [[], []]
    for v, axis, dim in ((a, a_axis, a_dim), (b, b_axis, b_dim)):
        here = lax.axis_index(axis)
        sums.append(lax.dynamic_index_in_dim(v, here, dim, keepdims=False))
    for step in (2, 1, 3):
        for n, (v, axis, dim) in enumerate(((a, a_axis, a_dim), (b, b_axis, b_dim))):
            here = lax.axis_index(axis)
            piece = lax.dynamic_index_in_dim(v, (here + step) % 4, dim, keepdims=False)
            if len(got[n]) == 2:
                piece = after(piece, got[n][0], *between)
            got[n].append(lax.ppermute(piece, axis, [(i, (i + step) % 4) for i in range(4)]))
    made = None
    if beside:
        made = beside(got[0][0], got[1][0])
        ready = lax.optimization_barrier((*sums, *got[0], *got[1], made))
        sums, got = ready[:2], (ready[2:5], ready[5:8])
    return [s + r[0] + r[1] + r[2] for s, r in zip(sums, got)], made


def body(x_share, w_share, g_share, fwd_a, fwd_b, fwd_c, bwd_a, bwd_b, bwd_c):
    x, w, g = x_share[0], w_share[0], g_share[0]
    fa, fb, fc = fwd_a[0], fwd_b[0], fwd_c[0]
    ba, bb, bc = bwd_a[0], bwd_b[0], bwd_c[0]
    party = lax.axis_index("party")
    party0 = party == 0
    first = party0.astype(F32)
    party_id = party.astype(jnp.int32).reshape(1)
    core_id = lax.axis_index("core").astype(jnp.int32).reshape(1)
    xl0 = lax.axis_index("xl") == 0
    ff = w.shape[1]

    x_mine0, x_mine1, x_theirs = turned(core_id, x)
    x0_mine = lax.ppermute(x_mine0, "party", SWAP)
    x_other = lax.ppermute(x_theirs, "core", SWAP)
    xs0 = jnp.concatenate([x_mine0, x_other[0]], axis=1)
    xs1 = jnp.concatenate([x_mine1, x_other[1]], axis=1)
    x0_other = lax.ppermute(x_other[0], "party", SWAP)
    x0 = jnp.concatenate([x0_mine, x0_other], axis=1)
    a_mine0, a_mine1, a_theirs = turned(core_id, after(ba, x_theirs))
    a_other = lax.ppermute(a_theirs, "core", SWAP)
    aa0 = jnp.concatenate([a_mine0, a_other[0]], axis=1)
    aa1 = jnp.concatenate([a_mine1, a_other[1]], axis=1)
    last = g[3 * g.shape[0] // 4 :]
    last = jnp.concatenate([last[:, : ff // 2], last[:, ff // 2 :]], axis=0)
    sent0 = jnp.where(party0, last, aa0)
    got0 = lax.ppermute(sent0, "party", SWAP)
    sent1 = jnp.concatenate(
        [
            xs1[:, :384],
            jnp.where(party0, xs1[:, 384:512], aa1[:, :128]),
            xs1[:, 512:896],
            jnp.where(party0, xs1[:, 896:], aa1[:, 512:640]),
            aa1[:, 128:384],
            aa1[:, 640:896],
        ],
        axis=1,
    )
    d = w - fb
    d_party = lax.ppermute(d, "party", SWAP)
    near = lax.ppermute(jnp.concatenate([fb, d], axis=1), "xl", SWAP)
    d_across = lax.ppermute(d, ("party", "xl"), [(0, 3), (3, 0), (1, 2), (2, 1)])
    d_party, near, d_across = lax.optimization_barrier((d_party, near, d_across, sent0, sent1))[:3]
    delta = d + d_party
    delta_near = near[:, ff:] + d_across
    packed = jnp.concatenate([fb + first * delta, delta], axis=1)
    packed_near = jnp.concatenate([near[:, :ff] + first * delta_near, delta_near], axis=1)
    weights = jnp.concatenate(
        [jnp.where(xl0, packed, packed_near), jnp.where(xl0, packed_near, packed)], axis=1
    )
    weights = lax.all_gather(after(weights, x0_mine), ("y", "z", "core"), axis=0, tiled=True)

    got1 = lax.ppermute(sent1, "party", SWAP)
    u_local = x - fa
    u = lax.ppermute(after(u_local, got0), "party", SWAP)

    g_other = lax.ppermute(after(g, a_other), "core", SWAP)
    b_other = lax.ppermute(after(bb, a_other), "core", SWAP)
    rights = (g, bb, g_other, b_other)
    early = grad_parts(party_id, after(xs0, u_local, xs1, aa1), aa0, (x0, got0), rights, (), 1)
    sent = (got0, lax.ppermute(after(got0, early), "core", SWAP))
    late = grad_parts(party_id, xs1, aa1, (got1,), rights, sent, LATE)

    early = lax.psum_scatter(early.reshape(16, 32, ff), ("z", "y"), scatter_dimension=0, tiled=True)
    early = early.reshape(2, 2, 8, ff)
    outputs = forward_call(local_kernel, (fa,), weights, 1, fc)
    part0, part1 = (part.reshape(4, 4, 16, ff) for part in late)

    def opened(*earlier):
        return forward_call(opened_kernel, (x, fa, u), weights, 0, after(outputs, *earlier))

    (part0, part1), y = scattered_pair(part0, "z", 0, part1, "y", 1, (outputs,), opened)
    (part0, part1), _ = scattered_pair(part0, "y", 0, part1, "z", 0)
    late = jnp.stack([part0, part1]).reshape(2, 2, 8, ff)
    both = jnp.concatenate([early, late], axis=2)
    spot = 2 * party + lax.axis_index("xl")

    def piece(at):
        return lax.dynamic_index_in_dim(both.reshape(4, *bc.shape), at % 4, 0, keepdims=False)

    grad = piece(spot) + first * bc
    for step in (2, 1, 3):
        give = piece(spot + step)
        if step == 2:
            give = give - first * bc
        grad = grad + lax.ppermute(
            give, ("party", "xl"), [(i, (i + step) % 4) for i in range(4)]
        )

    return (y[None], grad[None])


def solution(mesh):
    split = Mesh(
        mesh.devices.reshape(mesh.shape["party"], 4, 2, 4, 2),
        ("party", *DP),
    )
    spec = P("party", DP, None)
    return jax.shard_map(
        body, mesh=split, in_specs=(spec,) * 9, out_specs=(spec, spec), check_vma=False
    )
```

```python
import jax
import jax.numpy as jnp
from jax import lax
from jax.experimental import pallas as pl
from jax.experimental.pallas import tpu as pltpu
from jax.sharding import Mesh
from jax.sharding import PartitionSpec as P

DP = ("y", "xl", "z", "core")
SWAP = [(0, 1), (1, 0)]
F32 = jnp.float32
BF16 = jnp.bfloat16
SMEM = pl.BlockSpec(memory_space=pltpu.SMEM)
TILE = 512
LATE, BESIDE = 8, 1


def cost(flops, *arrays, weight=1):
    moved = sum(4 * a.size for a in arrays)
    return pl.CostEstimate(
        flops=weight * flops, bytes_accessed=weight * moved, transcendentals=0
    )


def params():
    return pltpu.CompilerParams(vmem_limit_bytes=56 * 1024 * 1024)


def after(value, *earlier):
    return lax.optimization_barrier((value, *earlier))[0]


def halves(a):
    high = a.astype(BF16)
    return high, (a - high.astype(F32)).astype(BF16)


def dot(left, right):
    return jnp.dot(left, right, preferred_element_type=F32)


def turn_kernel(core_ref, x_ref, a_ref, x_mine0, x_mine1, a_mine0, a_mine1, theirs):
    even = core_ref[0] == 0
    for n, (src, mines) in enumerate(((x_ref, (x_mine0, x_mine1)), (a_ref, (a_mine0, a_mine1)))):
        t = src[...].T
        for y in range(x_mine0.shape[1]):
            for xl in range(2):
                for z in range(4):
                    for k, mine in enumerate(mines):
                        at = (2 * y + xl) * 128 + z * 32 + k * 8
                        e, o = t[at : at + 8], t[at + 16 : at + 24]
                        mine[z, y, xl] = jnp.where(even, e, o)
                        theirs[n, k, z, y, xl] = jnp.where(even, o, e)


def turned(core, x, a):
    tokens = x.shape[0]
    mine = jax.ShapeDtypeStruct((4, 4, 2, 8, tokens), F32)
    mine_spec = pl.BlockSpec((4, 2, 2, 8, tokens), lambda i: (0, i, 0, 0, 0))
    theirs_spec = pl.BlockSpec((2, 2, 4, 2, 2, 8, tokens), lambda i: (0, 0, 0, i, 0, 0, 0))
    source = pl.BlockSpec((tokens, 512), lambda i: (0, i))
    *mines, theirs = pl.pallas_call(
        turn_kernel,
        grid=(2,),
        in_specs=[SMEM, source, source],
        out_specs=[mine_spec] * 4 + [theirs_spec],
        out_shape=[mine] * 4 + [jax.ShapeDtypeStruct((2, 2, *mine.shape), F32)],
        cost_estimate=cost(0, x, x, a, a),
        compiler_params=params(),
    )(core, x, a)
    rows = 128 * 2
    return [m.reshape(rows, tokens) for m in mines], theirs.reshape(2, 2, rows, tokens)


def passes(stack, right):
    rows = stack.shape[0] // 2
    high, low = halves(right)
    both = dot(stack[...], high)
    return both[:rows] + both[rows:] + dot(stack[:rows], low)


def grad_kernel(split, p_ref, x_ref, a_ref, *refs):
    pair, pair_sent, single = refs[-3:]
    outs, refs = (refs[-5:-3], refs[:-5]) if split else (refs[-4:-3], refs[:-4])
    got_refs, refs = (refs[:1], refs[1:]) if split else (refs[:3], refs[3:])
    g_ref, b_ref, go_ref, bo_ref = refs[:4]
    sent_refs = refs[4:]
    is_first = p_ref[0] == 0

    @pl.when(pl.program_id(0) == 0)
    def _():
        x, a = x_ref[...], a_ref[...]
        if split:
            got, late = got_refs[0][:, :1024], got_refs[0][:, 1024:]
            col = lax.broadcasted_iota(jnp.int32, x.shape, 1)
            kept = jnp.logical_or(jnp.logical_not(is_first), col % 512 < 384)
            zero = jnp.zeros((256, 128), F32)
            second = [got[:, 384:512], late[:, :256], zero, got[:, 896:], late[:, 256:], zero]
            second = jnp.where(is_first, jnp.concatenate(second, axis=1), a)
            got = jnp.where(kept, got, 0.0)
            a_sent = jnp.concatenate([a[:, 384:512], a[:, 896:]], axis=1)
            x_sent = jnp.concatenate([x[:, 384:512], x[:, 896:]], axis=1)
            pair_sent[:256], pair_sent[512:768] = halves(x_sent - a_sent)
            pair_sent[256:512], pair_sent[768:] = halves(a_sent)
        else:
            got = jnp.concatenate([got_refs[0][...], got_refs[1][...]], axis=1)
            second = jnp.where(is_first, got_refs[2][...], a)
        opened = x + got
        pair[:256], pair[512:768] = halves(opened - second)
        pair[256:512], pair[768:] = halves(second)
        single[:256], single[256:] = halves(jnp.where(is_first, a, opened))

    b, bo = b_ref[...], bo_ref[...]
    r = g_ref[...] - jnp.where(is_first, 0.0, b)
    ro = go_ref[...] - jnp.where(is_first, 0.0, bo)
    both = passes(pair, jnp.concatenate([r, ro], axis=0))
    if split:
        sent = jnp.concatenate([ref[...] for ref in sent_refs], axis=0)
        both += passes(pair_sent, jnp.where(is_first, 0.0, sent))
    shared = passes(single, jnp.concatenate([b, bo], axis=0))
    part0 = both[:256] - jnp.where(is_first, shared, 0.0)
    part1 = both[256:] + shared
    for n, part in enumerate((part0, part1)):
        part = part.reshape(16, 16, part.shape[1])
        if split:
            outs[n][...] = part
        else:
            outs[0][:, n] = part


def grad_parts(party, x, a, got, rights, sent, weight):
    tokens, ff = rights[0].shape
    lefts = (x, a, *got)
    right = pl.BlockSpec((tokens, TILE), lambda n: (0, n))
    per = 1024 // TILE
    part = pl.BlockSpec((128, TILE), lambda n: (n // per, n % per))
    return pl.pallas_call(
        lambda *refs: grad_kernel(bool(sent), *refs),
        grid=(ff // TILE,),
        in_specs=[SMEM]
        + [pl.BlockSpec(v.shape, lambda n: (0, 0)) for v in lefts]
        + [right] * 4
        + [part] * len(sent),
        out_specs=[pl.BlockSpec((16, 16, TILE), lambda n: (0, 0, n))] * 2
        if sent
        else pl.BlockSpec((16, 2, 16, TILE), lambda n: (0, 0, 0, n)),
        out_shape=[jax.ShapeDtypeStruct((16, 16, ff), F32)] * 2
        if sent
        else jax.ShapeDtypeStruct((16, 2, 16, ff), F32),
        scratch_shapes=[
            pltpu.VMEM((1024, 2 * tokens), BF16),
            pltpu.VMEM((1024, 256), BF16),
            pltpu.VMEM((512, 2 * tokens), BF16),
        ],
        cost_estimate=cost(3 * 2 * 768 * 2 * tokens * ff, *rights, *lefts, rights[0], weight=weight),
        compiler_params=params(),
    )(party, *lefts, *rights, *sent)


def store_split(value, stack):
    rows = value.shape[0]
    for xl in range(2):
        cols = [value[:, (2 * y + xl) * 128 :][:, :128] for y in range(4)]
        at = slice(xl * 512, xl * 512 + 512)
        stack[:rows, at], stack[rows:, at] = halves(jnp.concatenate(cols, axis=1))


def add_product(c_ref, w0_ref, w1_ref, out, stack):
    w = jnp.concatenate([w0_ref[...], w1_ref[...]], axis=0)
    out[...] = c_ref[...] + passes(stack, w)


def local_kernel(a_ref, w0_ref, w1_ref, c_ref, out, stack):
    @pl.when(pl.program_id(0) == 0)
    def _():
        store_split(a_ref[...], stack)

    add_product(c_ref, w0_ref, w1_ref, out, stack)


def opened_kernel(x_ref, a_ref, got_ref, w0_ref, w1_ref, c_ref, out, stack):
    @pl.when(pl.program_id(0) == 0)
    def _():
        store_split((x_ref[...] - a_ref[...]) + got_ref[...], stack)

    add_product(c_ref, w0_ref, w1_ref, out, stack)


def forward_call(kernel, lefts, weights, at, c):
    rows, ff = c.shape
    d = lefts[0].shape[1]
    steps = ff // TILE
    tile = pl.BlockSpec((rows, TILE), lambda n: (0, n))
    return pl.pallas_call(
        kernel,
        grid=(steps,),
        in_specs=[pl.BlockSpec((rows, d), lambda n: (0, 0))] * len(lefts)
        + [
            pl.BlockSpec((d // 2, TILE), lambda n: (0, at * steps + n)),
            pl.BlockSpec((d // 2, TILE), lambda n: (0, (at + 2) * steps + n)),
            tile,
        ],
        out_specs=tile,
        out_shape=jax.ShapeDtypeStruct(c.shape, F32),
        scratch_shapes=[pltpu.VMEM((2 * rows, d), BF16)],
        cost_estimate=cost(3 * 2 * rows * d * ff, weights, c, weight=BESIDE),
        compiler_params=params(),
    )(*lefts, weights, weights, c)


def scattered_pair(a, a_axis, a_dim, b, b_axis, b_dim, between=(), beside=None):
    sums, got = [], [[], []]
    for v, axis, dim in ((a, a_axis, a_dim), (b, b_axis, b_dim)):
        here = lax.axis_index(axis)
        sums.append(lax.dynamic_index_in_dim(v, here, dim, keepdims=False))
    for step in (2, 1, 3):
        for n, (v, axis, dim) in enumerate(((a, a_axis, a_dim), (b, b_axis, b_dim))):
            here = lax.axis_index(axis)
            piece = lax.dynamic_index_in_dim(v, (here + step) % 4, dim, keepdims=False)
            if len(got[n]) == 2:
                piece = after(piece, got[n][0], *between)
            got[n].append(lax.ppermute(piece, axis, [(i, (i + step) % 4) for i in range(4)]))
    made = None
    if beside:
        made = beside(got[0][0], got[1][0])
        ready = lax.optimization_barrier((*sums, *got[0], *got[1], made))
        sums, got = ready[:2], (ready[2:5], ready[5:8])
    return [s + r[0] + r[1] + r[2] for s, r in zip(sums, got)], made


def body(x_share, w_share, g_share, fwd_a, fwd_b, fwd_c, bwd_a, bwd_b, bwd_c):
    x, w, g = x_share[0], w_share[0], g_share[0]
    fa, fb, fc = fwd_a[0], fwd_b[0], fwd_c[0]
    ba, bb, bc = bwd_a[0], bwd_b[0], bwd_c[0]
    party = lax.axis_index("party")
    party0 = party == 0
    first = party0.astype(F32)
    party_id = party.astype(jnp.int32).reshape(1)
    core_id = lax.axis_index("core").astype(jnp.int32).reshape(1)
    xl0 = lax.axis_index("xl") == 0
    ff = w.shape[1]

    (x_mine0, x_mine1, a_mine0, a_mine1), theirs = turned(core_id, x, ba)
    x0_mine = lax.ppermute(x_mine0, "party", SWAP)
    other = lax.ppermute(theirs, "core", SWAP)
    x_other, a_other = other[0], other[1]
    xs0 = jnp.concatenate([x_mine0, x_other[0]], axis=1)
    xs1 = jnp.concatenate([x_mine1, x_other[1]], axis=1)
    x0_other = lax.ppermute(x_other[0], "party", SWAP)
    aa0 = jnp.concatenate([a_mine0, a_other[0]], axis=1)
    aa1 = jnp.concatenate([a_mine1, a_other[1]], axis=1)
    last = g[3 * g.shape[0] // 4 :]
    last = jnp.concatenate([last[:, : ff // 2], last[:, ff // 2 :]], axis=0)
    sent0 = jnp.where(party0, last, aa0)
    got0 = lax.ppermute(sent0, "party", SWAP)
    sent1 = jnp.concatenate(
        [
            xs1[:, :384],
            jnp.where(party0, xs1[:, 384:512], aa1[:, :128]),
            xs1[:, 512:896],
            jnp.where(party0, xs1[:, 896:], aa1[:, 512:640]),
            aa1[:, 128:384],
            aa1[:, 640:896],
        ],
        axis=1,
    )
    d = w - fb
    d_party = lax.ppermute(d, "party", SWAP)
    near = lax.ppermute(jnp.concatenate([fb, d], axis=1), "xl", SWAP)
    d_across = lax.ppermute(d, ("party", "xl"), [(0, 3), (3, 0), (1, 2), (2, 1)])
    d_party, near, d_across = lax.optimization_barrier((d_party, near, d_across, sent0, sent1))[:3]
    delta = d + d_party
    delta_near = near[:, ff:] + d_across
    packed = jnp.concatenate([fb + first * delta, delta], axis=1)
    packed_near = jnp.concatenate([near[:, :ff] + first * delta_near, delta_near], axis=1)
    weights = jnp.concatenate(
        [jnp.where(xl0, packed, packed_near), jnp.where(xl0, packed_near, packed)], axis=1
    )
    weights = lax.all_gather(after(weights, x0_mine), ("y", "z", "core"), axis=0, tiled=True)

    got1 = lax.ppermute(sent1, "party", SWAP)
    u_local = x - fa
    u = lax.ppermute(after(u_local, got0), "party", SWAP)

    g_other = lax.ppermute(after(g, other), "core", SWAP)
    b_other = lax.ppermute(after(bb, other), "core", SWAP)
    rights = (g, bb, g_other, b_other)
    early = grad_parts(party_id, after(xs0, u_local, xs1, aa1), aa0, (x0_mine, x0_other, got0), rights, (), 1)
    sent = (got0, lax.ppermute(after(got0, early), "core", SWAP))
    late = grad_parts(party_id, xs1, aa1, (got1,), rights, sent, LATE)

    early = lax.psum_scatter(early.reshape(16, 32, ff), ("z", "y"), scatter_dimension=0, tiled=True)
    early = early.reshape(2, 2, 8, ff)
    outputs = forward_call(local_kernel, (fa,), weights, 1, fc)
    part0, part1 = (part.reshape(4, 4, 16, ff) for part in late)

    def opened(*earlier):
        return forward_call(opened_kernel, (x, fa, u), weights, 0, after(outputs, *earlier))

    (part0, part1), y = scattered_pair(part0, "z", 0, part1, "y", 1, (outputs,), opened)
    (part0, part1), _ = scattered_pair(part0, "y", 0, part1, "z", 0)
    late = jnp.stack([part0, part1]).reshape(2, 2, 8, ff)
    both = jnp.concatenate([early, late], axis=2)
    spot = 2 * party + lax.axis_index("xl")

    def piece(at):
        return lax.dynamic_index_in_dim(both.reshape(4, *bc.shape), at % 4, 0, keepdims=False)

    grad = piece(spot) + first * bc
    for step in (2, 1, 3):
        give = piece(spot + step)
        if step == 2:
            give = give - first * bc
        grad = grad + lax.ppermute(
            give, ("party", "xl"), [(i, (i + step) % 4) for i in range(4)]
        )

    return (y[None], grad[None])


def solution(mesh):
    split = Mesh(
        mesh.devices.reshape(mesh.shape["party"], 4, 2, 4, 2),
        ("party", *DP),
    )
    spec = P("party", DP, None)
    return jax.shard_map(
        body, mesh=split, in_specs=(spec,) * 9, out_specs=(spec, spec), check_vma=False
    )
```

```python
import jax
import jax.numpy as jnp
from jax import lax
from jax.experimental import pallas as pl
from jax.experimental.pallas import tpu as pltpu
from jax.sharding import Mesh
from jax.sharding import PartitionSpec as P

DP = ("y", "xl", "z", "core")
SWAP = [(0, 1), (1, 0)]
F32 = jnp.float32
BF16 = jnp.bfloat16
SMEM = pl.BlockSpec(memory_space=pltpu.SMEM)
TILE = 512
LATE, BESIDE = 8, 1


def cost(flops, *arrays, weight=1):
    moved = sum(4 * a.size for a in arrays)
    return pl.CostEstimate(
        flops=weight * flops, bytes_accessed=weight * moved, transcendentals=0
    )


def params():
    return pltpu.CompilerParams(vmem_limit_bytes=56 * 1024 * 1024)


def after(value, *earlier):
    return lax.optimization_barrier((value, *earlier))[0]


def halves(a):
    high = a.astype(BF16)
    return high, (a - high.astype(F32)).astype(BF16)


def dot(left, right):
    return jnp.dot(left, right, preferred_element_type=F32)


def turn_kernel(core_ref, x_ref, a_ref, x_mine0, x_mine1, a_mine0, a_mine1, theirs):
    even = core_ref[0] == 0
    for n, (src, mines) in enumerate(((x_ref, (x_mine0, x_mine1)), (a_ref, (a_mine0, a_mine1)))):
        t = src[...].T
        for y in range(x_mine0.shape[1]):
            for xl in range(2):
                for z in range(4):
                    for k, mine in enumerate(mines):
                        at = (2 * y + xl) * 128 + z * 32 + k * 8
                        e, o = t[at : at + 8], t[at + 16 : at + 24]
                        mine[z, y, xl] = jnp.where(even, e, o)
                        theirs[n, k, z, y, xl] = jnp.where(even, o, e)


def turned(core, x, a):
    tokens = x.shape[0]
    mine = jax.ShapeDtypeStruct((4, 4, 2, 8, tokens), F32)
    mine_spec = pl.BlockSpec((4, 2, 2, 8, tokens), lambda i: (0, i, 0, 0, 0))
    theirs_spec = pl.BlockSpec((2, 2, 4, 2, 2, 8, tokens), lambda i: (0, 0, 0, i, 0, 0, 0))
    source = pl.BlockSpec((tokens, 512), lambda i: (0, i))
    *mines, theirs = pl.pallas_call(
        turn_kernel,
        grid=(2,),
        in_specs=[SMEM, source, source],
        out_specs=[mine_spec] * 4 + [theirs_spec],
        out_shape=[mine] * 4 + [jax.ShapeDtypeStruct((2, 2, *mine.shape), F32)],
        cost_estimate=cost(0, x, x, a, a),
        compiler_params=params(),
    )(core, x, a)
    rows = 128 * 2
    return [m.reshape(rows, tokens) for m in mines], theirs.reshape(2, 2, rows, tokens)


def passes(stack, right):
    rows = stack.shape[0] // 2
    high, low = halves(right)
    both = dot(stack[...], high)
    return both[:rows] + both[rows:] + dot(stack[:rows], low)


def grad_kernel(split, p_ref, x_ref, a_ref, *refs):
    pair, pair_sent, single = refs[-3:]
    outs, refs = (refs[-5:-3], refs[:-5]) if split else (refs[-4:-3], refs[:-4])
    got_refs, refs = (refs[:1], refs[1:]) if split else (refs[:3], refs[3:])
    g_ref, b_ref, go_ref, bo_ref = refs[:4]
    sent_refs = refs[4:]
    is_first = p_ref[0] == 0

    @pl.when(pl.program_id(0) == 0)
    def _():
        x, a = x_ref[...], a_ref[...]
        if split:
            got, late = got_refs[0][:, :1024], got_refs[0][:, 1024:]
            col = lax.broadcasted_iota(jnp.int32, x.shape, 1)
            kept = jnp.logical_or(jnp.logical_not(is_first), col % 512 < 384)
            zero = jnp.zeros((256, 128), F32)
            second = [got[:, 384:512], late[:, :256], zero, got[:, 896:], late[:, 256:], zero]
            second = jnp.where(is_first, jnp.concatenate(second, axis=1), a)
            got = jnp.where(kept, got, 0.0)
            a_sent = jnp.concatenate([a[:, 384:512], a[:, 896:]], axis=1)
            x_sent = jnp.concatenate([x[:, 384:512], x[:, 896:]], axis=1)
            pair_sent[:256], pair_sent[512:768] = halves(x_sent - a_sent)
            pair_sent[256:512], pair_sent[768:] = halves(a_sent)
        else:
            got = jnp.concatenate([got_refs[0][...], got_refs[1][...]], axis=1)
            second = jnp.where(is_first, got_refs[2][...], a)
        opened = x + got
        pair[:256], pair[512:768] = halves(opened - second)
        pair[256:512], pair[768:] = halves(second)
        single[:256], single[256:] = halves(jnp.where(is_first, a, opened))

    b, bo = b_ref[...], bo_ref[...]
    r = g_ref[...] - jnp.where(is_first, 0.0, b)
    ro = go_ref[...] - jnp.where(is_first, 0.0, bo)
    both = passes(pair, jnp.concatenate([r, ro], axis=0))
    if split:
        sent = jnp.concatenate([ref[...] for ref in sent_refs], axis=0)
        both += passes(pair_sent, jnp.where(is_first, 0.0, sent))
    shared = passes(single, jnp.concatenate([b, bo], axis=0))
    part0 = both[:256] - jnp.where(is_first, shared, 0.0)
    part1 = both[256:] + shared
    for n, part in enumerate((part0, part1)):
        part = part.reshape(16, 16, part.shape[1])
        if split:
            outs[n][...] = part
        else:
            outs[0][:, n] = part


def grad_parts(party, x, a, got, rights, sent, weight):
    tokens, ff = rights[0].shape
    lefts = (x, a, *got)
    right = pl.BlockSpec((tokens, TILE), lambda n: (0, n))
    per = 1024 // TILE
    part = pl.BlockSpec((128, TILE), lambda n: (n // per, n % per))
    return pl.pallas_call(
        lambda *refs: grad_kernel(bool(sent), *refs),
        grid=(ff // TILE,),
        in_specs=[SMEM]
        + [pl.BlockSpec(v.shape, lambda n: (0, 0)) for v in lefts]
        + [right] * 4
        + [part] * len(sent),
        out_specs=[pl.BlockSpec((16, 16, TILE), lambda n: (0, 0, n))] * 2
        if sent
        else pl.BlockSpec((16, 2, 16, TILE), lambda n: (0, 0, 0, n)),
        out_shape=[jax.ShapeDtypeStruct((16, 16, ff), F32)] * 2
        if sent
        else jax.ShapeDtypeStruct((16, 2, 16, ff), F32),
        scratch_shapes=[
            pltpu.VMEM((1024, 2 * tokens), BF16),
            pltpu.VMEM((1024, 256), BF16),
            pltpu.VMEM((512, 2 * tokens), BF16),
        ],
        cost_estimate=cost(3 * 2 * 768 * 2 * tokens * ff, *rights, *lefts, rights[0], weight=weight),
        compiler_params=params(),
    )(party, *lefts, *rights, *sent)


def store_split(value, stack):
    rows = value.shape[0]
    for xl in range(2):
        cols = [value[:, (2 * y + xl) * 128 :][:, :128] for y in range(4)]
        at = slice(xl * 512, xl * 512 + 512)
        stack[:rows, at], stack[rows:, at] = halves(jnp.concatenate(cols, axis=1))


def add_product(c_ref, w0_ref, w1_ref, out, stack):
    w = jnp.concatenate([w0_ref[...], w1_ref[...]], axis=0)
    out[...] = c_ref[...] + passes(stack, w)


def local_kernel(a_ref, w0_ref, w1_ref, c_ref, out, stack):
    @pl.when(pl.program_id(0) == 0)
    def _():
        store_split(a_ref[...], stack)

    add_product(c_ref, w0_ref, w1_ref, out, stack)


def opened_kernel(x_ref, a_ref, got_ref, w0_ref, w1_ref, c_ref, out, stack):
    @pl.when(pl.program_id(0) == 0)
    def _():
        store_split((x_ref[...] - a_ref[...]) + got_ref[...], stack)

    add_product(c_ref, w0_ref, w1_ref, out, stack)


def forward_call(kernel, lefts, weights, at, c):
    rows, ff = c.shape
    d = lefts[0].shape[1]
    steps = ff // TILE
    tile = pl.BlockSpec((rows, TILE), lambda n: (0, n))
    return pl.pallas_call(
        kernel,
        grid=(steps,),
        in_specs=[pl.BlockSpec((rows, d), lambda n: (0, 0))] * len(lefts)
        + [
            pl.BlockSpec((d // 2, TILE), lambda n: (0, at * steps + n)),
            pl.BlockSpec((d // 2, TILE), lambda n: (0, (at + 2) * steps + n)),
            tile,
        ],
        out_specs=tile,
        out_shape=jax.ShapeDtypeStruct(c.shape, F32),
        scratch_shapes=[pltpu.VMEM((2 * rows, d), BF16)],
        cost_estimate=cost(3 * 2 * rows * d * ff, weights, c, weight=BESIDE),
        compiler_params=params(),
    )(*lefts, weights, weights, c)


def scattered_pair(a, a_axis, a_dim, b, b_axis, b_dim, between=(), beside=None):
    sums, got = [], [[], []]
    for v, axis, dim in ((a, a_axis, a_dim), (b, b_axis, b_dim)):
        here = lax.axis_index(axis)
        sums.append(lax.dynamic_index_in_dim(v, here, dim, keepdims=False))
    for step in (2, 1, 3):
        for n, (v, axis, dim) in enumerate(((a, a_axis, a_dim), (b, b_axis, b_dim))):
            here = lax.axis_index(axis)
            piece = lax.dynamic_index_in_dim(v, (here + step) % 4, dim, keepdims=False)
            if len(got[n]) == 2:
                piece = after(piece, got[n][0], *between)
            got[n].append(lax.ppermute(piece, axis, [(i, (i + step) % 4) for i in range(4)]))
    made = None
    if beside:
        made = beside(got[0][0], got[1][0])
        ready = lax.optimization_barrier((*sums, *got[0], *got[1], made))
        sums, got = ready[:2], (ready[2:5], ready[5:8])
    return [s + r[0] + r[1] + r[2] for s, r in zip(sums, got)], made


def body(x_share, w_share, g_share, fwd_a, fwd_b, fwd_c, bwd_a, bwd_b, bwd_c):
    x, w, g = x_share[0], w_share[0], g_share[0]
    fa, fb, fc = fwd_a[0], fwd_b[0], fwd_c[0]
    ba, bb, bc = bwd_a[0], bwd_b[0], bwd_c[0]
    party = lax.axis_index("party")
    party0 = party == 0
    first = party0.astype(F32)
    party_id = party.astype(jnp.int32).reshape(1)
    core_id = lax.axis_index("core").astype(jnp.int32).reshape(1)
    xl0 = lax.axis_index("xl") == 0
    ff = w.shape[1]

    (x_mine0, x_mine1, a_mine0, a_mine1), theirs = turned(core_id, x, ba)
    x0_mine = lax.ppermute(x_mine0, "party", SWAP)
    other = lax.ppermute(theirs, "core", SWAP)
    x_other, a_other = other[0], other[1]
    xs0 = jnp.concatenate([x_mine0, x_other[0]], axis=1)
    xs1 = jnp.concatenate([x_mine1, x_other[1]], axis=1)
    x0_other = lax.ppermute(x_other[0], "party", SWAP)
    aa0 = jnp.concatenate([a_mine0, a_other[0]], axis=1)
    aa1 = jnp.concatenate([a_mine1, a_other[1]], axis=1)
    last = g[3 * g.shape[0] // 4 :]
    last = jnp.concatenate([last[:, : ff // 2], last[:, ff // 2 :]], axis=0)
    sent0 = jnp.where(party0, last, aa0)
    got0 = lax.ppermute(sent0, "party", SWAP)
    sent1 = jnp.concatenate(
        [
            xs1[:, :384],
            jnp.where(party0, xs1[:, 384:512], aa1[:, :128]),
            xs1[:, 512:896],
            jnp.where(party0, xs1[:, 896:], aa1[:, 512:640]),
            aa1[:, 128:384],
            aa1[:, 640:896],
        ],
        axis=1,
    )
    d = w - fb
    d_party = lax.ppermute(d, "party", SWAP)
    near = lax.ppermute(jnp.concatenate([fb, d], axis=1), "xl", SWAP)
    d_across = lax.ppermute(d, ("party", "xl"), [(0, 3), (3, 0), (1, 2), (2, 1)])
    d_party, near, d_across = lax.optimization_barrier((d_party, near, d_across, sent0, sent1))[:3]
    delta = d + d_party
    delta_near = near[:, ff:] + d_across
    packed = jnp.concatenate([fb + first * delta, delta], axis=1)
    packed_near = jnp.concatenate([near[:, :ff] + first * delta_near, delta_near], axis=1)
    weights = jnp.concatenate(
        [jnp.where(xl0, packed, packed_near), jnp.where(xl0, packed_near, packed)], axis=1
    )
    weights = lax.all_gather(after(weights, x0_mine), ("y", "z", "core"), axis=0, tiled=True)

    got1 = lax.ppermute(sent1, "party", SWAP)
    u_local = x - fa

    g_other = lax.ppermute(after(g, other), "core", SWAP)
    b_other = lax.ppermute(after(bb, other), "core", SWAP)
    rights = (g, bb, g_other, b_other)
    early = grad_parts(party_id, after(xs0, u_local, xs1, aa1), aa0, (x0_mine, x0_other, got0), rights, (), 1)
    sent = (got0, lax.ppermute(after(got0, early), "core", SWAP))
    u = lax.ppermute(after(u_local, sent[1]), "party", SWAP)
    late = grad_parts(party_id, xs1, aa1, (got1,), rights, sent, LATE)

    early = lax.psum_scatter(early.reshape(16, 32, ff), ("z", "y"), scatter_dimension=0, tiled=True)
    early = early.reshape(2, 2, 8, ff)
    outputs = forward_call(local_kernel, (fa,), weights, 1, fc)
    part0, part1 = (part.reshape(4, 4, 16, ff) for part in late)

    def opened(*earlier):
        return forward_call(opened_kernel, (x, fa, u), weights, 0, after(outputs, *earlier))

    (part0, part1), y = scattered_pair(part0, "z", 0, part1, "y", 1, (outputs,), opened)
    (part0, part1), _ = scattered_pair(part0, "y", 0, part1, "z", 0)
    late = jnp.stack([part0, part1]).reshape(2, 2, 8, ff)
    both = jnp.concatenate([early, late], axis=2)
    spot = 2 * party + lax.axis_index("xl")

    def piece(at):
        return lax.dynamic_index_in_dim(both.reshape(4, *bc.shape), at % 4, 0, keepdims=False)

    grad = piece(spot) + first * bc
    for step in (2, 1, 3):
        give = piece(spot + step)
        if step == 2:
            give = give - first * bc
        grad = grad + lax.ppermute(
            give, ("party", "xl"), [(i, (i + step) % 4) for i in range(4)]
        )

    return (y[None], grad[None])


def solution(mesh):
    split = Mesh(
        mesh.devices.reshape(mesh.shape["party"], 4, 2, 4, 2),
        ("party", *DP),
    )
    spec = P("party", DP, None)
    return jax.shard_map(
        body, mesh=split, in_specs=(spec,) * 9, out_specs=(spec, spec), check_vma=False
    )
```
